512 devices in a mesh: ctx: 16 (over z, core), ch: 32 (over x, y).
Axes of the slice: x: 4, y: 8, z: 8, core: 2. Of those that a mesh axis runs over, the one named last changes fastest.
Arguments:
- features: bfloat16 [3, 4096, 8192], P(None, 'ctx', 'ch'), may hold values from -6 to 6
- short_weight: float32 [3, 7, 8192], P(None, None, 'ch'), may hold values from -2 to 2
- rates: float32 [8192, 16], P('ch'), may hold values from 7.324219e-05 to 0.08
- residues: float32 [8192, 16], P('ch'), may hold values from -0.75 to 0.75
- skip: float32 [8192], P('ch'), may hold values from -4 to 4
- out_weight: bfloat16 [8192, 8192], P('ctx', 'ch'), may hold values from -0.0625 to 0.0625
Outputs:
- mixed: bfloat16 [4096, 8192], P('ctx', 'ch')
The draws below stay inside these ranges and needn't reach their ends.
All inputs are finite; a program needn't handle non-finite values.
Results may differ from the reference program's by a relative error of at most 0.0076.
Values may be sent and summed in bfloat16 or wider, within the bound.
No kernel may reach another device: no remote copies, remote signals or barrier semaphores. Data moves between devices by JAX's collectives and lax.ppermute only.
A program may use at most 64 MiB of HBM per device.

```python
import math
import jax
import jax.numpy as jnp
from jax import lax

D = 8192
MODES = 16
WIDTH = 7
TOKENS = 4096


def block_levels(own_key, extent, cuts, least, top_value):
    def one(dim, blocks):
        heights = jax.random.uniform(jax.random.fold_in(jax.random.fold_in(own_key, 6), dim), (blocks,), jnp.float32, least / len(cuts), top_value / len(cuts))
        return jnp.repeat(jnp.exp(heights), extent[dim] // blocks).reshape((-1,) + (1,) * (len(extent) - dim - 1))

    gain = one(*cuts[0])
    for cut in cuts[1:]:
        gain = gain * one(*cut)
    return gain


def noise(key, dims, deviation, limit, shards=(), kind=jnp.bfloat16):
    factor_of = block_levels(key, dims, shards, -0.22, 0.18) if shards else 1.0
    result = jax.random.normal(key, dims, jnp.float32) * deviation * factor_of
    return jnp.minimum(jnp.maximum(result, -limit), limit).astype(kind)


def setup_inputs(seed: int = 0) -> dict:
    splits = jax.random.split(jax.random.key(seed), 7)
    features = noise(splits[0], (3, TOKENS, D), 1.0, 6.0, ((1, 16), (2, 32)))
    short_weight = noise(splits[1], (3, WIDTH, D), WIDTH ** -0.5, 2.0, ((2, 32),), jnp.float32)
    rates = jnp.clip(jnp.exp(math.log(0.08) - 6.9960103 * jax.random.uniform(splits[2], (D, MODES), jnp.float32) ** block_levels(splits[2], (D, MODES), ((0, 32),), -0.2, 0.2)), 7.324219041038305e-05, 0.08)
    residues = noise(splits[3], (D, MODES), 0.05, 0.75, ((0, 32),), jnp.float32)
    skip = noise(splits[4], (D,), 1.0, 4.0, ((0, 32),), jnp.float32)
    out_weight = noise(splits[5], (D, D), D ** -0.5, 0.0625, ((0, 16), (1, 32)))
    return dict(features=features, short_weight=short_weight, rates=rates, residues=residues, skip=skip, out_weight=out_weight)


def reference(features, short_weight, rates, residues, skip, out_weight):
    inputs = features.astype(jnp.float32)
    padded = jnp.pad(inputs, ((0, 0), (WIDTH - 1, 0), (0, 0)))
    featured = jnp.zeros_like(inputs)
    for offset in range(WIDTH):
        featured = featured + short_weight[:, offset][:, None, :] * padded[:, WIDTH - 1 - offset:WIDTH - 1 - offset + TOKENS, :]
    featured = featured.astype(jnp.bfloat16)
    query = featured[0].astype(jnp.float32)
    product = (featured[1].astype(jnp.float32) * featured[2].astype(jnp.float32)).astype(jnp.bfloat16)
    product_value = product.astype(jnp.float32)
    group_size = math.gcd(D, 256)
    group_count = D // group_size
    positions = jnp.arange(TOKENS, dtype=jnp.float32)
    fft_length = 2 * TOKENS

    def convolve(block):
        rate_block, gain_block, signal = block
        kernel = jnp.einsum("cn,cnt->ct", gain_block, jnp.exp(-rate_block[:, :, None] * positions[None, None, :]), precision=lax.Precision.HIGHEST)
        spectrum = jnp.fft.rfft(signal.T, n=fft_length) * jnp.fft.rfft(kernel, n=fft_length)
        return jnp.fft.irfft(spectrum, n=fft_length)[:, :TOKENS].T

    signals = product_value.reshape(TOKENS, group_count, group_size).transpose(1, 0, 2)
    convolved = lax.map(convolve, (rates.reshape(group_count, group_size, MODES), residues.reshape(group_count, group_size, MODES), signals))
    convolved = convolved.transpose(1, 0, 2).reshape(TOKENS, D)
    conv_value = convolved + skip[None, :] * product_value
    gated = (query * conv_value).astype(jnp.bfloat16)
    return jnp.dot(gated, out_weight, preferred_element_type=jnp.float32).astype(jnp.bfloat16)
```

```python
import functools

import jax
import jax.numpy as jnp
from jax import lax
from jax.experimental import pallas as pl
from jax.experimental.pallas import tpu as pltpu
from jax.sharding import Mesh
from jax.sharding import PartitionSpec as P

STRETCH = 64
RIM = 8
SHAPE = {"c": 2, "x": 4}
F32 = jnp.float32
BF16 = jnp.bfloat16
CTX = ("z", "c")
CH = ("x", "y")
VMEM = pl.BlockSpec(memory_space=pltpu.VMEM)
SMEM = pl.BlockSpec(memory_space=pltpu.SMEM)


def local_kernel(features, rim, taps, rates, gains, skip, query, inner, before, totals, extended, product):
    streams, rows, chans = features.shape
    width = taps.shape[1]
    modes = rates.shape[0]
    stretches = rows // STRETCH
    piece = 32
    for f in range(streams):
        extended[f, 0:RIM, :] = rim[f].astype(F32)
        extended[f, RIM : RIM + rows, :] = features[f].astype(F32)
    for start in range(0, rows, piece):
        parts = []
        for f in range(streams):
            total = jnp.zeros((piece, chans), F32)
            for offset in range(width):
                at = RIM + start - offset
                total = total + taps[f, offset : offset + 1, :] * extended[f, at : at + piece, :]
            parts.append(total.astype(BF16))
        query[start : start + piece, :] = parts[0]
        product[start : start + piece, :] = (
            (parts[1].astype(F32) * parts[2].astype(F32)).astype(BF16).astype(F32)
        )
    decay = jnp.exp(-rates[...])
    gain = gains[...]
    through = skip[...]

    def eight(i, states):
        states = list(states)
        base = pl.multiple_of(i * 8, 8)
        for k in range(stretches):
            at = pl.multiple_of(k * STRETCH + base, 8)
            tile = product[pl.ds(at, 8), :]
            outs = []
            state = states[k]
            for r in range(8):
                state = decay * state + jnp.broadcast_to(tile[r : r + 1, :], (modes, chans))
                outs.append(jnp.sum(gain * state, axis=0, keepdims=True))
            states[k] = state
            inner[pl.ds(at, 8), :] = jnp.concatenate(outs, axis=0) + through * tile
        return tuple(states)

    zero = jnp.zeros((modes, chans), F32)
    states = lax.fori_loop(0, STRETCH // 8, eight, (zero,) * stretches)
    across = jnp.exp(-rates[...] * STRETCH)
    running = zero
    for k in range(stretches):
        before[k] = running
        running = across * running + states[k]
    for i in range(totals.shape[0]):
        totals[i] = running


def join_kernel(place, everyone, before, inner, query, table, rates, out, starts, gated):
    length, modes, chans = everyone.shape
    stretches = before.shape[0]
    rows = inner.shape[0]
    me = place[0]
    span = jnp.exp(-rates[...] * rows)
    incoming = jnp.zeros((modes, chans), F32)
    for i in range(length):
        incoming = jnp.where(i < me, span * incoming + everyone[i], incoming)
    for k in range(stretches):
        starts[k] = jnp.exp(-rates[...] * (k * STRETCH)) * incoming + before[k]

    def eight(i, carry):
        base = pl.multiple_of(i * 8, 8)
        totals = [inner[pl.ds(pl.multiple_of(k * STRETCH + base, 8), 8), :] for k in range(stretches)]
        for n in range(modes):
            weight = table[n, pl.ds(base, 8), :]
            for k in range(stretches):
                totals[k] = totals[k] + weight * starts[k, n : n + 1, :]
        for k in range(stretches):
            at = pl.multiple_of(k * STRETCH + base, 8)
            gated[pl.ds(at, 8), :] = query[pl.ds(at, 8), :].astype(F32) * totals[k]
        return carry

    lax.fori_loop(0, STRETCH // 8, eight, 0)
    turned = gated[...].T.astype(BF16)
    blocks = out.shape[0]
    height = out.shape[2]
    for b in range(blocks):
        for copy in range(out.shape[1]):
            out[b, copy] = turned[b * height : (b + 1) * height, :]


def project_kernel(gated, weight, out):
    depth = gated.shape[0] * gated.shape[1]
    left = gated[...].reshape(depth, gated.shape[2])
    right = weight[...].reshape(depth, weight.shape[3])
    out[0] = lax.dot_general(left, right, (((0,), (0,)), ((), ())), preferred_element_type=F32).astype(BF16)


def call(kernel, out_shape, scratch, flops, moved, in_specs, name):
    return pl.pallas_call(
        kernel,
        out_shape=out_shape,
        in_specs=in_specs,
        out_specs=jax.tree.map(lambda _: VMEM, out_shape),
        scratch_shapes=scratch,
        cost_estimate=pl.CostEstimate(flops=flops, bytes_accessed=moved, transcendentals=0),
        compiler_params=pltpu.CompilerParams(vmem_limit_bytes=32 << 20),
        name=name,
    )


def per_device(features, short_weight, rates, residues, skip, out_weight):
    streams, rows, chans = features.shape
    modes = rates.shape[1]
    length = lax.axis_size(CTX)
    xs, ys = lax.axis_size("x"), lax.axis_size("y")
    place = lax.axis_index(CTX)
    decay_rate = rates.T
    mode_gain = residues.T
    shape = jax.ShapeDtypeStruct

    rim = lax.ppermute(features[:, rows - RIM :, :], CTX, [(i, i + 1) for i in range(length - 1)])

    deep, wide = out_weight.shape
    owned = deep // chans
    piece = chans // xs
    sliced = out_weight.reshape(owned, xs, piece, wide).transpose(1, 0, 2, 3).reshape(xs, owned * piece, wide)
    sliced = lax.all_to_all(sliced, "x", split_axis=0, concat_axis=0, tiled=True)
    weights = lax.all_gather(sliced, CTX, axis=0, tiled=False)

    lag = jnp.arange(STRETCH, dtype=F32) + 1.0
    table = mode_gain[:, None, :] * jnp.exp(-decay_rate[:, None, :] * lag[None, :, None])
    rim, sliced, table = lax.optimization_barrier((rim, sliced, table))

    stretches = rows // STRETCH
    query, inner, before, totals = call(
        local_kernel,
        (
            shape((rows, chans), BF16),
            shape((rows, chans), F32),
            shape((stretches, modes, chans), F32),
            shape((length, modes, chans), F32),
        ),
        [pltpu.VMEM((streams, rows + RIM, chans), F32), pltpu.VMEM((rows, chans), F32)],
        8_000_000,
        2_000_000,
        [VMEM] * 6,
        "local",
    )(features, rim, short_weight, decay_rate, mode_gain, skip[None, :])
    everyone = lax.all_to_all(totals, CTX, split_axis=0, concat_axis=0, tiled=True)
    spread = call(
        join_kernel,
        shape((xs, ys, piece, rows), BF16),
        [pltpu.VMEM((stretches, modes, chans), F32), pltpu.VMEM((rows, chans), F32)],
        4_000_000,
        4_000_000,
        [SMEM] + [VMEM] * 6,
        "join",
    )(place.astype(jnp.int32).reshape(1), everyone, before, inner, query, table, decay_rate)
    gathered = lax.all_to_all(
        spread.reshape(xs * ys, piece, rows), CH, split_axis=0, concat_axis=0, tiled=True
    )
    partial = pl.pallas_call(
        project_kernel,
        out_shape=shape((xs, rows, wide), BF16),
        grid=(xs,),
        in_specs=[
            pl.BlockSpec((xs * ys, piece, rows), lambda i: (0, 0, 0)),
            pl.BlockSpec((length, 1, owned * piece, wide), lambda i: (0, i, 0, 0)),
        ],
        out_specs=pl.BlockSpec((1, rows, wide), lambda i: (i, 0, 0)),
        cost_estimate=pl.CostEstimate(
            flops=2 * rows * xs * ys * piece * wide * xs, bytes_accessed=6_000_000, transcendentals=0
        ),
        compiler_params=pltpu.CompilerParams(vmem_limit_bytes=32 << 20),
        name="project",
    )(gathered, weights)
    shares = lax.all_to_all(partial, "x", split_axis=0, concat_axis=0, tiled=True)
    total = shares[0].astype(F32)
    for i in range(1, xs):
        total = total + shares[i].astype(F32)
    return total.astype(BF16)


def solution(mesh):
    cores, xs = SHAPE["c"], SHAPE["x"]
    fine = Mesh(mesh.devices.reshape(-1, cores, xs, mesh.shape["ch"] // xs), ("z", "c", "x", "y"))
    return jax.shard_map(
        per_device,
        mesh=fine,
        in_specs=(
            P(None, CTX, CH),
            P(None, None, CH),
            P(CH, None),
            P(CH, None),
            P(CH),
            P(CTX, CH),
        ),
        out_specs=P(CTX, CH),
        check_vma=False,
    )
```

```python
import jax
import jax.numpy as jnp
from jax import lax
from jax.experimental import pallas as pl
from jax.experimental.pallas import tpu as pltpu
from jax.sharding import Mesh
from jax.sharding import PartitionSpec as P


STRETCH = 64
RIM = 8
SHAPE = {"c": 2, "x": 4}
F32 = jnp.float32
BF16 = jnp.bfloat16
CTX = ("z", "c")
CH = ("x", "y")
VMEM = pl.BlockSpec(memory_space=pltpu.VMEM)
SMEM = pl.BlockSpec(memory_space=pltpu.SMEM)


def local_kernel(
    features_at, taps_at, rates_at, gains_at, skip_at, rim, query, inner, before, decays, totals,
    features, taps, rates, gains, skip, sems, extended, product,
):
    pairs = ((features_at, features), (taps_at, taps), (rates_at, rates), (gains_at, gains), (skip_at, skip))
    copies = [pltpu.make_async_copy(src, dst, sems.at[i]) for i, (src, dst) in enumerate(pairs)]
    for copy in copies:
        copy.start()
    for copy in copies:
        copy.wait()
    streams, rows, chans = features.shape
    width = taps.shape[1]
    modes = rates.shape[0]
    stretches = rows // STRETCH
    piece = 32
    for f in range(streams):
        extended[f, 0:RIM, :] = rim[f].astype(F32)
        extended[f, RIM : RIM + rows, :] = features[f].astype(F32)
    for start in range(0, rows, piece):
        parts = []
        for f in range(streams):
            total = jnp.zeros((piece, chans), F32)
            for offset in range(width):
                at = RIM + start - offset
                total = total + taps[f, offset : offset + 1, :] * extended[f, at : at + piece, :]
            parts.append(total.astype(BF16))
        query[start : start + piece, :] = parts[0]
        product[start : start + piece, :] = (
            (parts[1].astype(F32) * parts[2].astype(F32)).astype(BF16).astype(F32)
        )
    decay = jnp.exp(-rates[...])
    gain = gains[...]
    through = skip[...]

    def eight(i, states):
        states = list(states)
        base = pl.multiple_of(i * 8, 8)
        for k in range(stretches):
            at = pl.multiple_of(k * STRETCH + base, 8)
            tile = product[pl.ds(at, 8), :]
            outs = []
            state = states[k]
            for r in range(8):
                state = decay * state + jnp.broadcast_to(tile[r : r + 1, :], (modes, chans))
                outs.append(jnp.sum(gain * state, axis=0, keepdims=True))
            states[k] = state
            inner[pl.ds(at, 8), :] = jnp.concatenate(outs, axis=0) + through * tile
        return tuple(states)

    zero = jnp.zeros((modes, chans), F32)
    states = lax.fori_loop(0, STRETCH // 8, eight, (zero,) * stretches)
    for k in range(stretches + 1):
        decays[k] = jnp.exp(-rates[...] * (k * STRETCH))
    across = decays[1]
    running = zero
    for k in range(stretches):
        before[k] = running
        running = across * running + states[k]
    totals[...] = running


def join_kernel(place, everyone, pair, before, decays, inner, query, table, out, starts, gated):
    chips, modes, chans = everyone.shape
    stretches = before.shape[0]
    span = decays[stretches]
    chip_span = span * span
    incoming = jnp.zeros((modes, chans), F32)
    for i in range(chips):
        incoming = jnp.where(i < place[0], chip_span * incoming + everyone[i], incoming)
    incoming = jnp.where(place[1] > 0, span * incoming + pair[0], incoming)
    for k in range(stretches):
        starts[k] = decays[k] * incoming + before[k]

    def eight(i, carry):
        base = pl.multiple_of(i * 8, 8)
        totals = [inner[pl.ds(pl.multiple_of(k * STRETCH + base, 8), 8), :] for k in range(stretches)]
        for n in range(modes):
            weight = table[n, pl.ds(base, 8), :]
            for k in range(stretches):
                totals[k] = totals[k] + weight * starts[k, n : n + 1, :]
        for k in range(stretches):
            at = pl.multiple_of(k * STRETCH + base, 8)
            gated[pl.ds(at, 8), :] = query[pl.ds(at, 8), :].astype(F32) * totals[k]
        return carry

    lax.fori_loop(0, STRETCH // 8, eight, 0)
    turned = gated[...].T.astype(BF16)
    blocks = out.shape[0]
    height = out.shape[2]
    for b in range(blocks):
        for copy in range(out.shape[1]):
            out[b, copy] = turned[b * height : (b + 1) * height, :]


def project_kernel(gated, weight, out):
    depth = gated.shape[0] * gated.shape[1]
    left = gated[...].reshape(depth, gated.shape[2])
    right = weight[...].reshape(depth, weight.shape[3])
    out[0] = lax.dot_general(left, right, (((0,), (0,)), ((), ())), preferred_element_type=F32).astype(BF16)


def whole(value):
    return pl.BlockSpec(value.shape, lambda i: (0,) * value.ndim)


def mixed_of(features, short_weight, rates, residues, skip, out_weight):
    streams, rows, chans = features.shape
    modes = rates.shape[1]
    length = lax.axis_size(CTX)
    zs, xs, ys = lax.axis_size("z"), lax.axis_size("x"), lax.axis_size("y")
    place = jnp.stack([lax.axis_index("z"), lax.axis_index("c")]).astype(jnp.int32)
    decay_rate = rates.T
    mode_gain = residues.T
    shape = jax.ShapeDtypeStruct

    deep, wide = out_weight.shape
    owned = deep // chans
    piece = chans // xs
    height = owned * piece
    sliced = out_weight.reshape(owned, xs, piece, wide).transpose(1, 0, 2, 3).reshape(xs, height, wide)
    sliced = lax.all_to_all(sliced, "x", split_axis=0, concat_axis=0, tiled=True)
    weights = lax.all_gather(sliced, CTX, axis=0, tiled=False)

    rim = lax.ppermute(features[:, rows - RIM :, :], CTX, [(i, i + 1) for i in range(length - 1)])
    lag = jnp.arange(STRETCH, dtype=F32) + 1.0
    table = mode_gain[:, None, :] * jnp.exp(-decay_rate[:, None, :] * lag[None, :, None])
    rim, table, place = lax.optimization_barrier((rim, table, place))

    stretches = rows // STRETCH
    shapes = (
        shape((rows, chans), BF16),
        shape((rows, chans), F32),
        shape((stretches, modes, chans), F32),
        shape((stretches + 1, modes, chans), F32),
        shape((modes, chans), F32),
    )
    operands = (features, short_weight, decay_rate, mode_gain, skip[None, :])
    query, inner, before, decays, totals = pl.pallas_call(
        local_kernel,
        out_shape=shapes,
        in_specs=[pl.BlockSpec(memory_space=pltpu.HBM)] * len(operands) + [VMEM],
        out_specs=(VMEM,) * len(shapes),
        scratch_shapes=[pltpu.VMEM(v.shape, v.dtype) for v in operands]
        + [
            pltpu.SemaphoreType.DMA((len(operands),)),
            pltpu.VMEM((streams, rows + RIM, chans), F32),
            pltpu.VMEM((rows, chans), F32),
        ],
        cost_estimate=pl.CostEstimate(flops=8_000_000, bytes_accessed=2_000_000, transcendentals=0),
        compiler_params=pltpu.CompilerParams(vmem_limit_bytes=32 << 20),
        name="local",
    )(*operands, rim)
    pair = lax.all_gather(totals, "c", axis=0, tiled=False)
    chip = decays[stretches] * pair[0] + pair[1]
    everyone = lax.all_to_all(
        jnp.broadcast_to(chip[None], (zs, modes, chans)), "z", split_axis=0, concat_axis=0, tiled=True
    )
    spread = pl.pallas_call(
        join_kernel,
        out_shape=shape((xs, ys, piece, rows), BF16),
        in_specs=[SMEM] + [VMEM] * 7,
        out_specs=VMEM,
        scratch_shapes=[pltpu.VMEM((stretches, modes, chans), F32), pltpu.VMEM((rows, chans), F32)],
        cost_estimate=pl.CostEstimate(flops=4_000_000, bytes_accessed=4_000_000, transcendentals=0),
        compiler_params=pltpu.CompilerParams(vmem_limit_bytes=32 << 20),
        name="join",
    )(place, everyone, pair, before, decays, inner, query, table)
    gathered = lax.all_to_all(
        spread.reshape(xs * ys, piece, rows), CH, split_axis=0, concat_axis=0, tiled=True
    )
    partial = pl.pallas_call(
        project_kernel,
        out_shape=shape((xs, rows, wide), BF16),
        grid=(xs,),
        in_specs=[
            whole(gathered),
            pl.BlockSpec((length, 1, height, wide), lambda i: (0, i, 0, 0)),
        ],
        out_specs=pl.BlockSpec((1, rows, wide), lambda i: (i, 0, 0)),
        cost_estimate=pl.CostEstimate(
            flops=2 * rows * length * height * wide * xs, bytes_accessed=6_000_000, transcendentals=0
        ),
        compiler_params=pltpu.CompilerParams(vmem_limit_bytes=60 << 20),
        name="project",
    )(gathered, weights)
    shares = lax.all_to_all(partial, "x", split_axis=0, concat_axis=0, tiled=True)
    total = shares[0].astype(F32)
    for i in range(1, xs):
        total = total + shares[i].astype(F32)
    return total.astype(BF16)


def solution(mesh):
    cores, xs = SHAPE["c"], SHAPE["x"]
    fine = Mesh(mesh.devices.reshape(-1, cores, xs, mesh.shape["ch"] // xs), ("z", "c", "x", "y"))
    return jax.shard_map(
        mixed_of,
        mesh=fine,
        in_specs=(
            P(None, CTX, CH),
            P(None, None, CH),
            P(CH, None),
            P(CH, None),
            P(CH),
            P(CTX, CH),
        ),
        out_specs=P(CTX, CH),
        check_vma=False,
    )
```

```python
import jax
import jax.numpy as jnp
from jax import lax
from jax.experimental import pallas as pl
from jax.experimental.pallas import tpu as pltpu
from jax.sharding import Mesh
from jax.sharding import PartitionSpec as P


STRETCH = 64
TILE = 8
RIM = 8
SHAPE = {"c": 2, "x": 4}
F32 = jnp.float32
BF16 = jnp.bfloat16
CTX = ("z", "c")
CH = ("x", "y")
VMEM = pl.BlockSpec(memory_space=pltpu.VMEM)
SMEM = pl.BlockSpec(memory_space=pltpu.SMEM)


def local_kernel(
    features_at, taps_at, rates_at, gains_at, skip_at, rim, query, inner, before, decays, slope, totals,
    features, taps, rates, gains, skip, sems, extended, product,
):
    pairs = ((rates_at, rates), (gains_at, gains), (features_at, features), (taps_at, taps), (skip_at, skip))
    copies = [pltpu.make_async_copy(src, dst, sems.at[i]) for i, (src, dst) in enumerate(pairs)]
    for copy in copies:
        copy.start()
    streams, rows, chans = features.shape
    width = taps.shape[1]
    modes = rates.shape[0]
    stretches = rows // STRETCH
    for copy in copies[:2]:
        copy.wait()
    for k in range(stretches + 1):
        decays[k] = jnp.exp(-rates[...] * (k * STRETCH))
    decays[stretches + 1] = jnp.exp(-rates[...] * TILE)
    lags = lax.broadcasted_iota(jnp.int32, (TILE, chans), 0).astype(F32) + 1.0
    for n in range(modes):
        slope[n] = gains[n : n + 1, :] * jnp.exp(-rates[n : n + 1, :] * lags)
    for copy in copies[2:]:
        copy.wait()
    piece = 32
    for f in range(streams):
        extended[f, 0:RIM, :] = rim[f].astype(F32)
        extended[f, RIM : RIM + rows, :] = features[f].astype(F32)
    for start in range(0, rows, piece):
        parts = []
        for f in range(streams):
            total = jnp.zeros((piece, chans), F32)
            for offset in range(width):
                at = RIM + start - offset
                total = total + taps[f, offset : offset + 1, :] * extended[f, at : at + piece, :]
            parts.append(total.astype(BF16))
        query[start : start + piece, :] = parts[0]
        product[start : start + piece, :] = (
            (parts[1].astype(F32) * parts[2].astype(F32)).astype(BF16).astype(F32)
        )
    decay = jnp.exp(-rates[...])
    gain = gains[...]
    through = skip[...]

    def eight(i, states):
        states = list(states)
        base = pl.multiple_of(i * 8, 8)
        for k in range(stretches):
            at = pl.multiple_of(k * STRETCH + base, 8)
            tile = product[pl.ds(at, 8), :]
            outs = []
            state = states[k]
            for r in range(8):
                state = decay * state + jnp.broadcast_to(tile[r : r + 1, :], (modes, chans))
                outs.append(jnp.sum(gain * state, axis=0, keepdims=True))
            states[k] = state
            inner[pl.ds(at, 8), :] = jnp.concatenate(outs, axis=0) + through * tile
        return tuple(states)

    zero = jnp.zeros((modes, chans), F32)
    states = lax.fori_loop(0, STRETCH // 8, eight, (zero,) * stretches)
    across = decays[1]
    running = zero
    for k in range(stretches):
        before[k] = running
        running = across * running + states[k]
    totals[...] = running


def join_kernel(place, everyone, pair, before, decays, slope, inner, query, out, starts, gated, table):
    chips, modes, chans = everyone.shape
    stretches = before.shape[0]
    span = decays[stretches]
    chip_span = span * span
    incoming = jnp.zeros((modes, chans), F32)
    for i in range(chips):
        incoming = jnp.where(i < place[0], chip_span * incoming + everyone[i], incoming)
    incoming = jnp.where(place[1] > 0, span * incoming + pair[0], incoming)
    for k in range(stretches):
        starts[k] = decays[k] * incoming + before[k]

    table[...] = slope[...]

    def eight(i, carry):
        base = pl.multiple_of(i * 8, 8)
        totals = [inner[pl.ds(pl.multiple_of(k * STRETCH + base, 8), 8), :] for k in range(stretches)]
        for n in range(modes):
            weight = table[n]
            table[n] = weight * decays[stretches + 1, n : n + 1, :]
            for k in range(stretches):
                totals[k] = totals[k] + weight * starts[k, n : n + 1, :]
        for k in range(stretches):
            at = pl.multiple_of(k * STRETCH + base, 8)
            gated[pl.ds(at, 8), :] = query[pl.ds(at, 8), :].astype(F32) * totals[k]
        return carry

    lax.fori_loop(0, STRETCH // 8, eight, 0)
    turned = gated[...].T.astype(BF16)
    blocks = out.shape[0]
    height = out.shape[2]
    for b in range(blocks):
        for copy in range(out.shape[1]):
            out[b, copy] = turned[b * height : (b + 1) * height, :]


def project_kernel(gated, weight_at, out, weight, sems):
    parts = out.shape[0]
    copies = [pltpu.make_async_copy(weight_at.at[:, i], weight.at[i], sems.at[i]) for i in range(parts)]
    for copy in copies:
        copy.start()
    depth = gated.shape[0] * gated.shape[1]
    left = gated[...].reshape(depth, gated.shape[2]).T
    for i in range(parts):
        copies[i].wait()
        right = weight[i].reshape(depth, weight.shape[3])
        out[i] = jnp.dot(left, right, preferred_element_type=F32).astype(BF16)


def mixed_of(features, short_weight, rates, residues, skip, out_weight):
    streams, rows, chans = features.shape
    modes = rates.shape[1]
    length = lax.axis_size(CTX)
    zs, xs, ys = lax.axis_size("z"), lax.axis_size("x"), lax.axis_size("y")
    place = jnp.stack([lax.axis_index("z"), lax.axis_index("c")]).astype(jnp.int32)
    decay_rate = rates.T
    mode_gain = residues.T
    shape = jax.ShapeDtypeStruct

    deep, wide = out_weight.shape
    owned = deep // chans
    piece = chans // xs
    height = owned * piece
    sliced = out_weight.reshape(owned, xs, piece, wide).transpose(1, 0, 2, 3).reshape(xs, height, wide)
    sliced = lax.all_to_all(sliced, "x", split_axis=0, concat_axis=0, tiled=True)
    weights = lax.all_gather(sliced, CTX, axis=0, tiled=False)

    rim = lax.ppermute(features[:, rows - RIM :, :], CTX, [(i, i + 1) for i in range(length - 1)])
    rim, place = lax.optimization_barrier((rim, place))

    stretches = rows // STRETCH
    shapes = (
        shape((rows, chans), BF16),
        shape((rows, chans), F32),
        shape((stretches, modes, chans), F32),
        shape((stretches + 2, modes, chans), F32),
        shape((modes, TILE, chans), F32),
        shape((modes, chans), F32),
    )
    operands = (features, short_weight, decay_rate, mode_gain, skip[None, :])
    query, inner, before, decays, slope, totals = pl.pallas_call(
        local_kernel,
        out_shape=shapes,
        in_specs=[pl.BlockSpec(memory_space=pl.ANY)] * len(operands) + [VMEM],
        out_specs=(VMEM,) * len(shapes),
        scratch_shapes=[pltpu.VMEM(v.shape, v.dtype) for v in operands]
        + [
            pltpu.SemaphoreType.DMA((len(operands),)),
            pltpu.VMEM((streams, rows + RIM, chans), F32),
            pltpu.VMEM((rows, chans), F32),
        ],
        cost_estimate=pl.CostEstimate(flops=8_000_000, bytes_accessed=2_000_000, transcendentals=0),
        compiler_params=pltpu.CompilerParams(vmem_limit_bytes=60 << 20),
        name="local",
    )(*operands, rim)
    pair = lax.all_gather(totals, "c", axis=0, tiled=False)
    chip = decays[stretches] * pair[0] + pair[1]
    everyone = lax.all_to_all(
        jnp.broadcast_to(chip[None], (zs, modes, chans)), "z", split_axis=0, concat_axis=0, tiled=True
    )
    spread = pl.pallas_call(
        join_kernel,
        out_shape=shape((xs, ys, piece, rows), BF16),
        in_specs=[SMEM] + [VMEM] * 7,
        out_specs=VMEM,
        scratch_shapes=[
            pltpu.VMEM((stretches, modes, chans), F32),
            pltpu.VMEM((rows, chans), F32),
            pltpu.VMEM((modes, TILE, chans), F32),
        ],
        cost_estimate=pl.CostEstimate(flops=4_000_000, bytes_accessed=4_000_000, transcendentals=0),
        compiler_params=pltpu.CompilerParams(vmem_limit_bytes=32 << 20),
        name="join",
    )(place, everyone, pair, before, decays, slope, inner, query)
    gathered = lax.all_to_all(
        spread.reshape(xs * ys, piece, rows), CH, split_axis=0, concat_axis=0, tiled=True
    )
    partial = pl.pallas_call(
        project_kernel,
        out_shape=shape((xs, rows, wide), BF16),
        in_specs=[VMEM, pl.BlockSpec(memory_space=pl.ANY)],
        out_specs=VMEM,
        scratch_shapes=[
            pltpu.VMEM((xs, length, height, wide), BF16),
            pltpu.SemaphoreType.DMA((xs,)),
        ],
        cost_estimate=pl.CostEstimate(
            flops=2 * rows * length * height * wide * xs, bytes_accessed=6_000_000, transcendentals=0
        ),
        compiler_params=pltpu.CompilerParams(vmem_limit_bytes=58 << 20),
        name="project",
    )(gathered, weights)
    shares = lax.all_to_all(partial, "x", split_axis=0, concat_axis=0, tiled=True)
    total = shares[0].astype(F32)
    for i in range(1, xs):
        total = total + shares[i].astype(F32)
    return total.astype(BF16)


def solution(mesh):
    cores, xs = SHAPE["c"], SHAPE["x"]
    fine = Mesh(mesh.devices.reshape(-1, cores, xs, mesh.shape["ch"] // xs), ("z", "c", "x", "y"))
    return jax.shard_map(
        mixed_of,
        mesh=fine,
        in_specs=(
            P(None, CTX, CH),
            P(None, None, CH),
            P(CH, None),
            P(CH, None),
            P(CH),
            P(CTX, CH),
        ),
        out_specs=P(CTX, CH),
        check_vma=False,
    )
```

```python
import jax
import jax.numpy as jnp
from jax import lax
from jax.experimental import pallas as pl
from jax.experimental.pallas import tpu as pltpu
from jax.sharding import Mesh
from jax.sharding import PartitionSpec as P

STRETCH = 64
TILE = 8
RIM = 8
SHAPE = {"zl": 2, "c": 2, "x": 4, "yl": 2}
F32 = jnp.float32
BF16 = jnp.bfloat16
Z = ("zh", "zl")
CTX = ("zh", "zl", "c")
CH = ("x", "yh", "yl")
VMEM = pl.BlockSpec(memory_space=pltpu.VMEM)
SMEM = pl.BlockSpec(memory_space=pltpu.SMEM)


def local_kernel(features, table, rim, query, inner, before, decays, slope, totals, extended, product):
    streams, rows, chans = features.shape
    stretches, modes, _ = before.shape
    width = RIM - 1
    rates = table[0:modes, :]
    gain = table[modes : 2 * modes, :]
    first = 2 * modes
    through = table[first + width : first + RIM, :]
    for k in range(stretches + 1):
        decays[k] = jnp.exp(-rates * (k * STRETCH))
    decays[stretches + 1] = jnp.exp(-rates * TILE)
    lags = lax.broadcasted_iota(jnp.int32, (TILE, chans), 0).astype(F32) + 1.0
    for n in range(modes):
        slope[n] = gain[n : n + 1, :] * jnp.exp(-rates[n : n + 1, :] * lags)
    piece = 32
    for f in range(streams):
        extended[f, 0:RIM, :] = rim[f].astype(F32)
        extended[f, RIM : RIM + rows, :] = features[f].astype(F32)
    for start in range(0, rows, piece):
        parts = []
        for f in range(streams):
            total = jnp.zeros((piece, chans), F32)
            for offset in range(width):
                at = RIM + start - offset
                tap = first + f * RIM + offset
                total = total + table[tap : tap + 1, :] * extended[f, at : at + piece, :]
            parts.append(total.astype(BF16))
        query[start : start + piece, :] = parts[0]
        product[start : start + piece, :] = (
            (parts[1].astype(F32) * parts[2].astype(F32)).astype(BF16).astype(F32)
        )
    decay = jnp.exp(-rates)

    def eight(i, states):
        states = list(states)
        base = pl.multiple_of(i * TILE, TILE)
        for k in range(stretches):
            at = pl.multiple_of(k * STRETCH + base, TILE)
            tile = product[pl.ds(at, TILE), :]
            outs = []
            state = states[k]
            for r in range(TILE):
                state = decay * state + jnp.broadcast_to(tile[r : r + 1, :], (modes, chans))
                outs.append(jnp.sum(gain * state, axis=0, keepdims=True))
            states[k] = state
            inner[pl.ds(at, TILE), :] = jnp.concatenate(outs, axis=0) + through * tile
        return tuple(states)

    zero = jnp.zeros((modes, chans), F32)
    states = lax.fori_loop(0, STRETCH // TILE, eight, (zero,) * stretches)
    across = decays[1]
    running = zero
    for k in range(stretches):
        before[k] = running
        running = across * running + states[k]
    totals[...] = running


def join_kernel(place, everyone, pair, before, decays, slope, inner, query, out, starts, gated, table):
    chips, modes, chans = everyone.shape
    stretches = before.shape[0]
    span = decays[stretches]
    chip_span = span * span
    incoming = jnp.zeros((modes, chans), F32)
    for i in range(chips):
        incoming = jnp.where(i < place[0], chip_span * incoming + everyone[i], incoming)
    incoming = jnp.where(place[1] > 0, span * incoming + pair[0], incoming)
    for k in range(stretches):
        starts[k] = decays[k] * incoming + before[k]
    table[...] = slope[...]

    def eight(i, carry):
        base = pl.multiple_of(i * TILE, TILE)
        totals = [inner[pl.ds(pl.multiple_of(k * STRETCH + base, TILE), TILE), :] for k in range(stretches)]
        for n in range(modes):
            weight = table[n]
            table[n] = weight * decays[stretches + 1, n : n + 1, :]
            for k in range(stretches):
                totals[k] = totals[k] + weight * starts[k, n : n + 1, :]
        for k in range(stretches):
            at = pl.multiple_of(k * STRETCH + base, TILE)
            gated[pl.ds(at, TILE), :] = query[pl.ds(at, TILE), :].astype(F32) * totals[k]
        return carry

    lax.fori_loop(0, STRETCH // TILE, eight, 0)
    turned = gated[...].T.astype(BF16)
    for copy in range(out.shape[0]):
        out[copy] = turned


def project_kernel(place, own, other, parts, out, weight):
    core = place[1]
    zh, zl, blocks, height, half = parts.shape
    depth = zh * height
    for b in range(blocks):
        block = jnp.where(core == b, 0, 1)
        for i in range(zh):
            for l in range(zl):
                weight[i * height : (i + 1) * height, l * half : (l + 1) * half] = parts[i, l, block]
        right = weight[...]
        for left, core_of in ((own, core), (other, 1 - core)):
            left = left[...].reshape(depth, left.shape[2])
            total = lax.dot_general(left, right, (((0,), (0,)), ((), ())), preferred_element_type=F32)
            total = total.astype(BF16)
            for l in range(zl):
                out[(b * zl + l) * 2 + core_of] = total[:, l * half : (l + 1) * half]


def finish_kernel(shares, out):
    halves = 2
    half = shares.shape[2]
    for h in range(halves):
        total = shares[h].astype(F32)
        for i in range(1, shares.shape[0] // halves):
            total = total + shares[i * halves + h].astype(F32)
        out[:, h * half : (h + 1) * half] = total.astype(BF16)


def cost(flops, moved):
    return pl.CostEstimate(flops=flops, bytes_accessed=moved, transcendentals=0)


def per_device(features, short_weight, rates, residues, skip, out_weight):
    streams, rows, chans = features.shape
    modes = rates.shape[1]
    width = short_weight.shape[1]
    zh, zl, xs = lax.axis_size("zh"), lax.axis_size("zl"), lax.axis_size("x")
    yh, yl = lax.axis_size("yh"), lax.axis_size("yl")
    length = lax.axis_size(CTX)
    high = lax.axis_index("yh") // zl
    place = jnp.stack([lax.axis_index(Z), lax.axis_index("c")]).astype(jnp.int32)
    shape = jax.ShapeDtypeStruct
    limit = pltpu.CompilerParams(vmem_limit_bytes=32 << 20)

    deep, wide = out_weight.shape
    half = wide // 2
    low_half, high_half = out_weight[:, :half], out_weight[:, half:]
    routes = []
    for flip in (0, 1):
        pairs = []
        for q in range(zl * 2):
            for n in range(yh):
                core = (n // zl) ^ flip
                pairs.append((q * yh + n, ((n % zl) * 2 + core) * yh + q))
        value = jnp.where((high ^ flip) == 0, low_half, high_half)
        routes.append(lax.ppermute(value, ("zl", "c", "yh"), pairs))
    sliced = jnp.stack(routes)

    rim = lax.ppermute(features[:, rows - RIM :, :], CTX, [(i, i + 1) for i in range(length - 1)])
    blank = jnp.zeros((1, chans), F32)
    rest = [short_weight[0], skip[None, :]]
    for f in range(1, streams):
        rest += [short_weight[f], blank]
    table = jnp.concatenate([rates.T, residues.T] + rest, axis=0)
    rim, table, place = lax.optimization_barrier((rim, table, place))

    stretches = rows // STRETCH
    shapes = (
        shape((rows, chans), BF16),
        shape((rows, chans), F32),
        shape((stretches, modes, chans), F32),
        shape((stretches + 2, modes, chans), F32),
        shape((modes, TILE, chans), F32),
        shape((modes, chans), F32),
    )
    query, inner, before, decays, slope, totals = pl.pallas_call(
        local_kernel,
        out_shape=shapes,
        in_specs=[VMEM] * 3,
        out_specs=(VMEM,) * len(shapes),
        scratch_shapes=[pltpu.VMEM((streams, rows + RIM, chans), F32), pltpu.VMEM((rows, chans), F32)],
        cost_estimate=cost(8_000_000, 2_000_000),
        compiler_params=limit,
        name="local",
    )(features, table, rim)
    pair = lax.all_gather(totals, "c", axis=0, tiled=False)
    chip = decays[stretches] * pair[0] + pair[1]
    chip, sliced = lax.optimization_barrier((chip, sliced))
    weights = lax.all_gather(sliced, Z, axis=0, tiled=False)
    everyone = lax.all_to_all(
        jnp.broadcast_to(chip[None], (zh * zl, modes, chans)), Z, split_axis=0, concat_axis=0, tiled=True
    )
    spread = pl.pallas_call(
        join_kernel,
        out_shape=shape((xs * yl, chans, rows), BF16),
        in_specs=[SMEM] + [VMEM] * 7,
        out_specs=VMEM,
        scratch_shapes=[
            pltpu.VMEM((stretches, modes, chans), F32),
            pltpu.VMEM((rows, chans), F32),
            pltpu.VMEM((modes, TILE, chans), F32),
        ],
        cost_estimate=cost(4_000_000, 4_000_000),
        compiler_params=limit,
        name="join",
    )(place, everyone, pair, before, decays, slope, inner, query)
    own = lax.all_to_all(spread, ("x", "yl"), split_axis=0, concat_axis=0, tiled=True)
    other = lax.ppermute(own, "c", [(0, 1), (1, 0)])
    depth = xs * yl * chans
    partial = pl.pallas_call(
        project_kernel,
        out_shape=shape((yh * 2, rows, half), BF16),
        in_specs=[SMEM, VMEM, VMEM, VMEM],
        out_specs=VMEM,
        scratch_shapes=[pltpu.VMEM((depth, zl * half), BF16)],
        cost_estimate=cost(4 * rows * depth * half * yh, 6_000_000),
        compiler_params=pltpu.CompilerParams(vmem_limit_bytes=48 << 20),
        name="project",
    )(place, own, other, weights.reshape(zh, zl, 2, deep, half))
    shares = lax.all_to_all(partial, ("yh", "c"), split_axis=0, concat_axis=0, tiled=True)
    return pl.pallas_call(
        finish_kernel,
        out_shape=shape((rows, wide), BF16),
        in_specs=[VMEM],
        out_specs=VMEM,
        cost_estimate=cost(500_000, 700_000),
        compiler_params=limit,
        name="finish",
    )(shares)


def solution(mesh):
    zl, cores, xs, yl = (SHAPE[name] for name in ("zl", "c", "x", "yl"))
    zh = mesh.shape["ctx"] // (zl * cores)
    yh = mesh.shape["ch"] // (xs * yl)
    fine = Mesh(mesh.devices.reshape(zh, zl, cores, xs, yh, yl), CTX + CH)
    return jax.shard_map(
        per_device,
        mesh=fine,
        in_specs=(
            P(None, CTX, CH),
            P(None, None, CH),
            P(CH, None),
            P(CH, None),
            P(CH),
            P(CTX, CH),
        ),
        out_specs=P(CTX, CH),
        check_vma=False,
    )
```

```python
import jax
import jax.numpy as jnp
from jax import lax
from jax.experimental import pallas as pl
from jax.experimental.pallas import tpu as pltpu
from jax.sharding import Mesh
from jax.sharding import PartitionSpec as P


STRETCH = 64
TILE = 8
RIM = 8
SHAPE = {"c": 2, "x": 4}
F32 = jnp.float32
BF16 = jnp.bfloat16
CTX = ("z", "c")
CH = ("x", "y")
VMEM = pl.BlockSpec(memory_space=pltpu.VMEM)
SMEM = pl.BlockSpec(memory_space=pltpu.SMEM)


def local_kernel(
    features_at, taps_at, rates_at, gains_at, skip_at, rim, query, inner, before, decays, slope, totals,
    features, taps, rates_in, gains_in, skip, sems, extended, product,
):
    pairs = ((rates_at, rates_in), (gains_at, gains_in), (features_at, features), (taps_at, taps), (skip_at, skip))
    copies = [pltpu.make_async_copy(src, dst, sems.at[i]) for i, (src, dst) in enumerate(pairs)]
    for copy in copies:
        copy.start()
    streams, rows, chans = features.shape
    stretches, modes, _ = before.shape
    width = taps.shape[1]
    for copy in copies[:2]:
        copy.wait()
    rates = rates_in[...]
    gain = gains_in[...]
    for k in range(stretches + 1):
        decays[k] = jnp.exp(-rates * (k * STRETCH))
    decays[stretches + 1] = jnp.exp(-rates * TILE)
    lags = lax.broadcasted_iota(jnp.int32, (TILE, chans), 0).astype(F32) + 1.0
    for n in range(modes):
        slope[n] = gain[n : n + 1, :] * jnp.exp(-rates[n : n + 1, :] * lags)
    for copy in copies[2:]:
        copy.wait()
    through = skip[...]
    piece = 32
    for f in range(streams):
        extended[f, 0:RIM, :] = rim[f].astype(F32)
        extended[f, RIM : RIM + rows, :] = features[f].astype(F32)
    for start in range(0, rows, piece):
        parts = []
        for f in range(streams):
            total = jnp.zeros((piece, chans), F32)
            for offset in range(width):
                at = RIM + start - offset
                total = total + taps[f, offset : offset + 1, :] * extended[f, at : at + piece, :]
            parts.append(total.astype(BF16))
        query[start : start + piece, :] = parts[0]
        product[start : start + piece, :] = (
            (parts[1].astype(F32) * parts[2].astype(F32)).astype(BF16).astype(F32)
        )
    decay = jnp.exp(-rates)

    def eight(i, states):
        states = list(states)
        base = pl.multiple_of(i * TILE, TILE)
        for k in range(stretches):
            at = pl.multiple_of(k * STRETCH + base, TILE)
            tile = product[pl.ds(at, TILE), :]
            outs = []
            state = states[k]
            for r in range(TILE):
                state = decay * state + jnp.broadcast_to(tile[r : r + 1, :], (modes, chans))
                outs.append(jnp.sum(gain * state, axis=0, keepdims=True))
            states[k] = state
            inner[pl.ds(at, TILE), :] = jnp.concatenate(outs, axis=0) + through * tile
        return tuple(states)

    zero = jnp.zeros((modes, chans), F32)
    states = lax.fori_loop(0, STRETCH // TILE, eight, (zero,) * stretches)
    across = decays[1]
    running = zero
    for k in range(stretches):
        before[k] = running
        running = across * running + states[k]
    totals[...] = running


def join_kernel(place, everyone, pair, before, decays, slope, inner, query, out, starts, gated, table):
    chips, modes, chans = everyone.shape
    stretches = before.shape[0]
    span = decays[stretches]
    chip_span = span * span
    incoming = jnp.zeros((modes, chans), F32)
    for i in range(chips):
        incoming = jnp.where(i < place[0], chip_span * incoming + everyone[i], incoming)
    incoming = jnp.where(place[1] > 0, span * incoming + pair[0], incoming)
    for k in range(stretches):
        starts[k] = decays[k] * incoming + before[k]
    table[...] = slope[...]

    def eight(i, carry):
        base = pl.multiple_of(i * TILE, TILE)
        totals = [inner[pl.ds(pl.multiple_of(k * STRETCH + base, TILE), TILE), :] for k in range(stretches)]
        for n in range(modes):
            weight = table[n]
            table[n] = weight * decays[stretches + 1, n : n + 1, :]
            for k in range(stretches):
                totals[k] = totals[k] + weight * starts[k, n : n + 1, :]
        for k in range(stretches):
            at = pl.multiple_of(k * STRETCH + base, TILE)
            gated[pl.ds(at, TILE), :] = query[pl.ds(at, TILE), :].astype(F32) * totals[k]
        return carry

    lax.fori_loop(0, STRETCH // TILE, eight, 0)
    turned = gated[...].T.astype(BF16)
    blocks, copies, height, _ = out.shape
    for b in range(blocks):
        for copy in range(copies):
            out[b, copy] = turned[b * height : (b + 1) * height, :]


def project_kernel(gated, weight_at, out, weight, sems):
    parts = out.shape[0]
    copies = [pltpu.make_async_copy(weight_at.at[:, i], weight.at[i], sems.at[i]) for i in range(parts)]
    for copy in copies:
        copy.start()
    depth = gated.shape[0] * gated.shape[1]
    left = gated[...].reshape(depth, gated.shape[2])
    for i in range(parts):
        copies[i].wait()
        right = weight[i].reshape(depth, weight.shape[3])
        total = lax.dot_general(left, right, (((0,), (0,)), ((), ())), preferred_element_type=F32)
        out[i] = total.astype(BF16)


def mixed_of(features, short_weight, rates, residues, skip, out_weight):
    streams, rows, chans = features.shape
    modes = rates.shape[1]
    length = lax.axis_size(CTX)
    zs, xs, ys = lax.axis_size("z"), lax.axis_size("x"), lax.axis_size("y")
    place = jnp.stack([lax.axis_index("z"), lax.axis_index("c")]).astype(jnp.int32)
    decay_rate = rates.T
    mode_gain = residues.T
    shape = jax.ShapeDtypeStruct

    deep, wide = out_weight.shape
    owned = deep // chans
    piece = chans // xs
    height = owned * piece
    sliced = out_weight.reshape(owned, xs, piece, wide).transpose(1, 0, 2, 3).reshape(xs, height, wide)
    sliced = lax.all_to_all(sliced, "x", split_axis=0, concat_axis=0, tiled=True)
    weights = lax.all_gather(sliced, CTX, axis=0, tiled=False)

    rim = lax.ppermute(features[:, rows - RIM :, :], CTX, [(i, i + 1) for i in range(length - 1)])
    rim, place = lax.optimization_barrier((rim, place))

    stretches = rows // STRETCH
    shapes = (
        shape((rows, chans), BF16),
        shape((rows, chans), F32),
        shape((stretches, modes, chans), F32),
        shape((stretches + 2, modes, chans), F32),
        shape((modes, TILE, chans), F32),
        shape((modes, chans), F32),
    )
    operands = (features, short_weight, decay_rate, mode_gain, skip[None, :])
    operands = tuple(pltpu.with_memory_space_constraint(v, pltpu.HBM) for v in operands)
    query, inner, before, decays, slope, totals = pl.pallas_call(
        local_kernel,
        out_shape=shapes,
        in_specs=[pl.BlockSpec(memory_space=pltpu.HBM)] * len(operands) + [VMEM],
        out_specs=(VMEM,) * len(shapes),
        scratch_shapes=[pltpu.VMEM(v.shape, v.dtype) for v in operands]
        + [
            pltpu.SemaphoreType.DMA((len(operands),)),
            pltpu.VMEM((streams, rows + RIM, chans), F32),
            pltpu.VMEM((rows, chans), F32),
        ],
        cost_estimate=pl.CostEstimate(flops=8_000_000, bytes_accessed=2_000_000, transcendentals=0),
        compiler_params=pltpu.CompilerParams(vmem_limit_bytes=32 << 20),
        name="local",
    )(*operands, rim)
    pair = lax.all_gather(totals, "c", axis=0, tiled=False)
    chip = decays[stretches] * pair[0] + pair[1]
    everyone = lax.all_to_all(
        jnp.broadcast_to(chip[None], (zs, modes, chans)), "z", split_axis=0, concat_axis=0, tiled=True
    )
    spread = pl.pallas_call(
        join_kernel,
        out_shape=shape((xs, ys, piece, rows), BF16),
        in_specs=[SMEM] + [VMEM] * 7,
        out_specs=VMEM,
        scratch_shapes=[
            pltpu.VMEM((stretches, modes, chans), F32),
            pltpu.VMEM((rows, chans), F32),
            pltpu.VMEM((modes, TILE, chans), F32),
        ],
        cost_estimate=pl.CostEstimate(flops=4_000_000, bytes_accessed=4_000_000, transcendentals=0),
        compiler_params=pltpu.CompilerParams(vmem_limit_bytes=32 << 20),
        name="join",
    )(place, everyone, pair, before, decays, slope, inner, query)
    gathered = lax.all_to_all(
        spread.reshape(xs * ys, piece, rows), CH, split_axis=0, concat_axis=0, tiled=True
    )
    weights = pltpu.with_memory_space_constraint(weights.reshape(length, xs, height, wide), pltpu.HBM)
    partial = pl.pallas_call(
        project_kernel,
        out_shape=shape((xs, rows, wide), BF16),
        in_specs=[VMEM, pl.BlockSpec(memory_space=pl.ANY)],
        out_specs=VMEM,
        scratch_shapes=[pltpu.VMEM((xs, length, height, wide), BF16), pltpu.SemaphoreType.DMA((xs,))],
        cost_estimate=pl.CostEstimate(
            flops=2 * rows * xs * ys * piece * wide * xs, bytes_accessed=6_000_000, transcendentals=0
        ),
        compiler_params=pltpu.CompilerParams(vmem_limit_bytes=32 << 20),
        name="project",
    )(gathered, weights)
    shares = lax.all_to_all(partial, "x", split_axis=0, concat_axis=0, tiled=True)
    total = shares[0].astype(F32)
    for i in range(1, xs):
        total = total + shares[i].astype(F32)
    return total.astype(BF16)


def solution(mesh):
    cores, xs = SHAPE["c"], SHAPE["x"]
    fine = Mesh(mesh.devices.reshape(-1, cores, xs, mesh.shape["ch"] // xs), ("z", "c", "x", "y"))
    return jax.shard_map(
        mixed_of,
        mesh=fine,
        in_specs=(
            P(None, CTX, CH),
            P(None, None, CH),
            P(CH, None),
            P(CH, None),
            P(CH),
            P(CTX, CH),
        ),
        out_specs=P(CTX, CH),
        check_vma=False,
    )
```

```python
import jax
import jax.numpy as jnp
from jax import lax
from jax.experimental import pallas as pl
from jax.experimental.pallas import tpu as pltpu
from jax.sharding import Mesh
from jax.sharding import PartitionSpec as P


STRETCH = 64
TILE = 8
RIM = 8
SHAPE = {"c": 2, "x": 4, "yl": 2}
F32 = jnp.float32
BF16 = jnp.bfloat16
CTX = ("z", "c")
CH = ("x", "yh", "yl")
DEEP = ("x", "yl")
VMEM = pl.BlockSpec(memory_space=pltpu.VMEM)
SMEM = pl.BlockSpec(memory_space=pltpu.SMEM)


def local_kernel(
    features_at, taps_at, rates_at, gains_at, skip_at, rim, query, inner, before, decays, slope, totals,
    features, taps, rates_in, gains_in, skip, sems, extended, product,
):
    pairs = ((rates_at, rates_in), (gains_at, gains_in), (features_at, features), (taps_at, taps), (skip_at, skip))
    copies = [pltpu.make_async_copy(src, dst, sems.at[i]) for i, (src, dst) in enumerate(pairs)]
    for copy in copies:
        copy.start()
    streams, rows, chans = features.shape
    stretches, modes, _ = before.shape
    width = taps.shape[1]
    for copy in copies[:2]:
        copy.wait()
    rates = rates_in[...]
    gain = gains_in[...]
    for k in range(stretches + 1):
        decays[k] = jnp.exp(-rates * (k * STRETCH))
    decays[stretches + 1] = jnp.exp(-rates * TILE)
    lags = lax.broadcasted_iota(jnp.int32, (TILE, chans), 0).astype(F32) + 1.0
    for n in range(modes):
        slope[n] = gain[n : n + 1, :] * jnp.exp(-rates[n : n + 1, :] * lags)
    for copy in copies[2:]:
        copy.wait()
    through = skip[...]
    piece = 32
    for f in range(streams):
        extended[f, 0:RIM, :] = rim[f].astype(F32)
        extended[f, RIM : RIM + rows, :] = features[f].astype(F32)
    for start in range(0, rows, piece):
        parts = []
        for f in range(streams):
            total = jnp.zeros((piece, chans), F32)
            for offset in range(width):
                at = RIM + start - offset
                total = total + taps[f, offset : offset + 1, :] * extended[f, at : at + piece, :]
            parts.append(total.astype(BF16))
        query[start : start + piece, :] = parts[0]
        product[start : start + piece, :] = (
            (parts[1].astype(F32) * parts[2].astype(F32)).astype(BF16).astype(F32)
        )
    decay = jnp.exp(-rates)

    def eight(i, states):
        states = list(states)
        base = pl.multiple_of(i * TILE, TILE)
        for k in range(stretches):
            at = pl.multiple_of(k * STRETCH + base, TILE)
            tile = product[pl.ds(at, TILE), :]
            outs = []
            state = states[k]
            for r in range(TILE):
                state = decay * state + jnp.broadcast_to(tile[r : r + 1, :], (modes, chans))
                outs.append(jnp.sum(gain * state, axis=0, keepdims=True))
            states[k] = state
            inner[pl.ds(at, TILE), :] = jnp.concatenate(outs, axis=0) + through * tile
        return tuple(states)

    zero = jnp.zeros((modes, chans), F32)
    states = lax.fori_loop(0, STRETCH // TILE, eight, (zero,) * stretches)
    across = decays[1]
    running = zero
    for k in range(stretches):
        before[k] = running
        running = across * running + states[k]
    totals[...] = running


def join_kernel(place, everyone, pair, before, decays, slope, inner, query, out, starts, gated, table):
    chips, modes, chans = everyone.shape
    stretches = before.shape[0]
    span = decays[stretches]
    chip_span = span * span
    incoming = jnp.zeros((modes, chans), F32)
    for i in range(chips):
        incoming = jnp.where(i < place[0], chip_span * incoming + everyone[i], incoming)
    incoming = jnp.where(place[1] > 0, span * incoming + pair[0], incoming)
    for k in range(stretches):
        starts[k] = decays[k] * incoming + before[k]
    table[...] = slope[...]

    def eight(i, carry):
        base = pl.multiple_of(i * TILE, TILE)
        totals = [inner[pl.ds(pl.multiple_of(k * STRETCH + base, TILE), TILE), :] for k in range(stretches)]
        for n in range(modes):
            weight = table[n]
            table[n] = weight * decays[stretches + 1, n : n + 1, :]
            for k in range(stretches):
                totals[k] = totals[k] + weight * starts[k, n : n + 1, :]
        for k in range(stretches):
            at = pl.multiple_of(k * STRETCH + base, TILE)
            gated[pl.ds(at, TILE), :] = query[pl.ds(at, TILE), :].astype(F32) * totals[k]
        return carry

    lax.fori_loop(0, STRETCH // TILE, eight, 0)
    turned = gated[...].T.astype(BF16)
    outer, copies, inner_blocks, height, _ = out.shape
    for b in range(outer):
        for l in range(inner_blocks):
            at = (b * inner_blocks + l) * height
            for copy in range(copies):
                out[b, copy, l] = turned[at : at + height, :]


def project_kernel(gated, weight_at, out, weight, sems):
    parts = out.shape[0]
    groups, length, height, wide = weight.shape
    share = parts // groups
    single = wide // share
    copies = [
        pltpu.make_async_copy(
            weight_at.at[:, i],
            weight.at[i // share, :, :, pl.ds((i % share) * single, single)],
            sems.at[i],
        )
        for i in range(parts)
    ]
    for copy in copies:
        copy.start()
    depth = length * height
    left = gated[...].reshape(depth, gated.shape[2])
    for i in range(groups):
        for copy in copies[i * share : (i + 1) * share]:
            copy.wait()
        right = weight[i].reshape(depth, wide)
        total = lax.dot_general(left, right, (((0,), (0,)), ((), ())), preferred_element_type=F32)
        for j in range(share):
            out[i * share + j] = total[:, j * single : (j + 1) * single].astype(BF16)


def mixed_of(features, short_weight, rates, residues, skip, out_weight):
    streams, rows, chans = features.shape
    modes = rates.shape[1]
    length = lax.axis_size(CTX)
    zs, xs, yh, yl = (lax.axis_size(name) for name in ("z", "x", "yh", "yl"))
    splits = xs * yl
    place = jnp.stack([lax.axis_index("z"), lax.axis_index("c")]).astype(jnp.int32)
    decay_rate = rates.T
    mode_gain = residues.T
    shape = jax.ShapeDtypeStruct

    deep, wide = out_weight.shape
    owned = deep // chans
    piece = chans // splits
    height = owned * piece
    sliced = out_weight.reshape(owned, splits, piece, wide).transpose(1, 0, 2, 3)
    sliced = sliced.reshape(splits, height, wide)
    sliced = lax.all_to_all(sliced, DEEP, split_axis=0, concat_axis=0, tiled=True)
    weights = lax.all_gather(sliced, CTX, axis=0, tiled=False)

    rim = lax.ppermute(features[:, rows - RIM :, :], CTX, [(i, i + 1) for i in range(length - 1)])
    rim, place = lax.optimization_barrier((rim, place))

    stretches = rows // STRETCH
    shapes = (
        shape((rows, chans), BF16),
        shape((rows, chans), F32),
        shape((stretches, modes, chans), F32),
        shape((stretches + 2, modes, chans), F32),
        shape((modes, TILE, chans), F32),
        shape((modes, chans), F32),
    )
    operands = (features, short_weight, decay_rate, mode_gain, skip[None, :])
    operands = tuple(pltpu.with_memory_space_constraint(v, pltpu.HBM) for v in operands)
    query, inner, before, decays, slope, totals = pl.pallas_call(
        local_kernel,
        out_shape=shapes,
        in_specs=[pl.BlockSpec(memory_space=pltpu.HBM)] * len(operands) + [VMEM],
        out_specs=(VMEM,) * len(shapes),
        scratch_shapes=[pltpu.VMEM(v.shape, v.dtype) for v in operands]
        + [
            pltpu.SemaphoreType.DMA((len(operands),)),
            pltpu.VMEM((streams, rows + RIM, chans), F32),
            pltpu.VMEM((rows, chans), F32),
        ],
        cost_estimate=pl.CostEstimate(flops=8_000_000, bytes_accessed=2_000_000, transcendentals=0),
        compiler_params=pltpu.CompilerParams(vmem_limit_bytes=32 << 20),
        name="local",
    )(*operands, rim)
    pair = lax.all_gather(totals, "c", axis=0, tiled=False)
    chip = decays[stretches] * pair[0] + pair[1]
    everyone = lax.all_to_all(
        jnp.broadcast_to(chip[None], (zs, modes, chans)), "z", split_axis=0, concat_axis=0, tiled=True
    )
    spread = pl.pallas_call(
        join_kernel,
        out_shape=shape((xs, yh, yl, piece, rows), BF16),
        in_specs=[SMEM] + [VMEM] * 7,
        out_specs=VMEM,
        scratch_shapes=[
            pltpu.VMEM((stretches, modes, chans), F32),
            pltpu.VMEM((rows, chans), F32),
            pltpu.VMEM((modes, TILE, chans), F32),
        ],
        cost_estimate=pl.CostEstimate(flops=4_000_000, bytes_accessed=4_000_000, transcendentals=0),
        compiler_params=pltpu.CompilerParams(vmem_limit_bytes=32 << 20),
        name="join",
    )(place, everyone, pair, before, decays, slope, inner, query)
    gathered = lax.all_to_all(
        spread.reshape(xs * yh * yl, piece, rows), CH, split_axis=0, concat_axis=0, tiled=True
    )
    weights = pltpu.with_memory_space_constraint(weights.reshape(length, splits, height, wide), pltpu.HBM)
    partial = pl.pallas_call(
        project_kernel,
        out_shape=shape((splits, rows, wide), BF16),
        in_specs=[VMEM, pl.BlockSpec(memory_space=pl.ANY)],
        out_specs=VMEM,
        scratch_shapes=[
            pltpu.VMEM((splits // 2, length, height, 2 * wide), BF16),
            pltpu.SemaphoreType.DMA((splits,)),
        ],
        cost_estimate=pl.CostEstimate(
            flops=2 * rows * length * height * wide * splits, bytes_accessed=6_000_000, transcendentals=0
        ),
        compiler_params=pltpu.CompilerParams(vmem_limit_bytes=32 << 20),
        name="project",
    )(gathered, weights)
    shares = lax.all_to_all(partial, DEEP, split_axis=0, concat_axis=0, tiled=True)
    total = shares[0].astype(F32)
    for i in range(1, splits):
        total = total + shares[i].astype(F32)
    return total.astype(BF16)


def solution(mesh):
    cores, xs, yl = SHAPE["c"], SHAPE["x"], SHAPE["yl"]
    yh = mesh.shape["ch"] // (xs * yl)
    fine = Mesh(mesh.devices.reshape(-1, cores, xs, yh, yl), CTX + CH)
    return jax.shard_map(
        mixed_of,
        mesh=fine,
        in_specs=(
            P(None, CTX, CH),
            P(None, None, CH),
            P(CH, None),
            P(CH, None),
            P(CH),
            P(CTX, CH),
        ),
        out_specs=P(CTX, CH),
        check_vma=False,
    )
```

```python
import jax
import jax.numpy as jnp
from jax import lax
from jax.experimental import pallas as pl
from jax.experimental.pallas import tpu as pltpu
from jax.sharding import Mesh
from jax.sharding import PartitionSpec as P


STRETCH = 64
TILE = 8
RIM = 8
SHAPE = {"c": 2, "x": 4, "yl": 2}
F32 = jnp.float32
BF16 = jnp.bfloat16
CTX = ("z", "c")
CH = ("x", "yh", "yl")
DEEP = ("yl", "x")
VMEM = pl.BlockSpec(memory_space=pltpu.VMEM)
SMEM = pl.BlockSpec(memory_space=pltpu.SMEM)


def local_kernel(
    features_at, taps_at, rates_at, gains_at, skip_at, rim, query, inner, before, decays, slope, totals,
    features, taps, rates_in, gains_in, skip, sems, extended, product,
):
    pairs = ((rates_at, rates_in), (gains_at, gains_in), (features_at, features), (taps_at, taps), (skip_at, skip))
    copies = [pltpu.make_async_copy(src, dst, sems.at[i]) for i, (src, dst) in enumerate(pairs)]
    for copy in copies:
        copy.start()
    streams, rows, chans = features.shape
    stretches, modes, _ = before.shape
    width = taps.shape[1]
    for copy in copies[:2]:
        copy.wait()
    rates = rates_in[...]
    gain = gains_in[...]
    for k in range(stretches + 1):
        decays[k] = jnp.exp(-rates * (k * STRETCH))
    decays[stretches + 1] = jnp.exp(-rates * TILE)
    lags = lax.broadcasted_iota(jnp.int32, (TILE, chans), 0).astype(F32) + 1.0
    for n in range(modes):
        slope[n] = gain[n : n + 1, :] * jnp.exp(-rates[n : n + 1, :] * lags)
    for copy in copies[2:]:
        copy.wait()
    through = skip[...]
    piece = 32
    for f in range(streams):
        extended[f, 0:RIM, :] = rim[f].astype(F32)
        extended[f, RIM : RIM + rows, :] = features[f].astype(F32)
    for start in range(0, rows, piece):
        parts = []
        for f in range(streams):
            total = jnp.zeros((piece, chans), F32)
            for offset in range(width):
                at = RIM + start - offset
                total = total + taps[f, offset : offset + 1, :] * extended[f, at : at + piece, :]
            parts.append(total.astype(BF16))
        query[start : start + piece, :] = parts[0]
        product[start : start + piece, :] = (
            (parts[1].astype(F32) * parts[2].astype(F32)).astype(BF16).astype(F32)
        )
    decay = jnp.exp(-rates)

    def eight(i, states):
        states = list(states)
        base = pl.multiple_of(i * TILE, TILE)
        for k in range(stretches):
            at = pl.multiple_of(k * STRETCH + base, TILE)
            tile = product[pl.ds(at, TILE), :]
            outs = []
            state = states[k]
            for r in range(TILE):
                state = decay * state + jnp.broadcast_to(tile[r : r + 1, :], (modes, chans))
                outs.append(jnp.sum(gain * state, axis=0, keepdims=True))
            states[k] = state
            inner[pl.ds(at, TILE), :] = jnp.concatenate(outs, axis=0) + through * tile
        return tuple(states)

    zero = jnp.zeros((modes, chans), F32)
    states = lax.fori_loop(0, STRETCH // TILE, eight, (zero,) * stretches)
    across = decays[1]
    running = zero
    for k in range(stretches):
        before[k] = running
        running = across * running + states[k]
    totals[...] = running


def join_kernel(place, everyone, pair, before, decays, slope, inner, query, out, starts, gated, table):
    chips, modes, chans = everyone.shape
    stretches = before.shape[0]
    span = decays[stretches]
    chip_span = span * span
    incoming = jnp.zeros((modes, chans), F32)
    for i in range(chips):
        incoming = jnp.where(i < place[0], chip_span * incoming + everyone[i], incoming)
    incoming = jnp.where(place[1] > 0, span * incoming + pair[0], incoming)
    for k in range(stretches):
        starts[k] = decays[k] * incoming + before[k]
    table[...] = slope[...]

    def eight(i, carry):
        base = pl.multiple_of(i * TILE, TILE)
        totals = [inner[pl.ds(pl.multiple_of(k * STRETCH + base, TILE), TILE), :] for k in range(stretches)]
        for n in range(modes):
            weight = table[n]
            table[n] = weight * decays[stretches + 1, n : n + 1, :]
            for k in range(stretches):
                totals[k] = totals[k] + weight * starts[k, n : n + 1, :]
        for k in range(stretches):
            at = pl.multiple_of(k * STRETCH + base, TILE)
            gated[pl.ds(at, TILE), :] = query[pl.ds(at, TILE), :].astype(F32) * totals[k]
        return carry

    lax.fori_loop(0, STRETCH // TILE, eight, 0)
    turned = gated[...].T.astype(BF16)
    blocks, copies, height, _ = out.shape
    for b in range(blocks):
        for copy in range(copies):
            out[b, copy] = turned[b * height : (b + 1) * height, :]


def project_kernel(gated, weight_at, out, weight, sems):
    parts = out.shape[0]
    groups, length, height, wide = weight.shape
    share = parts // groups
    single = wide // share
    copies = [
        pltpu.make_async_copy(
            weight_at.at[:, i],
            weight.at[i // share, :, :, pl.ds((i % share) * single, single)],
            sems.at[i],
        )
        for i in range(parts)
    ]
    for copy in copies:
        copy.start()
    depth = length * height
    left = gated[...].reshape(depth, gated.shape[2])
    for i in range(groups):
        for copy in copies[i * share : (i + 1) * share]:
            copy.wait()
        right = weight[i].reshape(depth, wide)
        total = lax.dot_general(left, right, (((0,), (0,)), ((), ())), preferred_element_type=F32)
        for j in range(share):
            out[i * share + j] = total[:, j * single : (j + 1) * single].astype(BF16)


def mixed_of(features, short_weight, rates, residues, skip, out_weight):
    streams, rows, chans = features.shape
    modes = rates.shape[1]
    length = lax.axis_size(CTX)
    zs, xs, yh, yl = (lax.axis_size(name) for name in ("z", "x", "yh", "yl"))
    splits = xs * yl
    place = jnp.stack([lax.axis_index("z"), lax.axis_index("c")]).astype(jnp.int32)
    decay_rate = rates.T
    mode_gain = residues.T
    shape = jax.ShapeDtypeStruct

    deep, wide = out_weight.shape
    piece = chans // xs
    height = deep // splits
    sliced = out_weight.reshape(splits, height, wide)
    sliced = lax.all_to_all(sliced, DEEP, split_axis=0, concat_axis=0, tiled=True)
    weights = lax.all_gather(sliced, CTX, axis=0, tiled=False)

    rim = lax.ppermute(features[:, rows - RIM :, :], CTX, [(i, i + 1) for i in range(length - 1)])
    rim, place = lax.optimization_barrier((rim, place))

    stretches = rows // STRETCH
    shapes = (
        shape((rows, chans), BF16),
        shape((rows, chans), F32),
        shape((stretches, modes, chans), F32),
        shape((stretches + 2, modes, chans), F32),
        shape((modes, TILE, chans), F32),
        shape((modes, chans), F32),
    )
    operands = (features, short_weight, decay_rate, mode_gain, skip[None, :])
    operands = tuple(pltpu.with_memory_space_constraint(v, pltpu.HBM) for v in operands)
    query, inner, before, decays, slope, totals = pl.pallas_call(
        local_kernel,
        out_shape=shapes,
        in_specs=[pl.BlockSpec(memory_space=pltpu.HBM)] * len(operands) + [VMEM],
        out_specs=(VMEM,) * len(shapes),
        scratch_shapes=[pltpu.VMEM(v.shape, v.dtype) for v in operands]
        + [
            pltpu.SemaphoreType.DMA((len(operands),)),
            pltpu.VMEM((streams, rows + RIM, chans), F32),
            pltpu.VMEM((rows, chans), F32),
        ],
        cost_estimate=pl.CostEstimate(flops=8_000_000, bytes_accessed=2_000_000, transcendentals=0),
        compiler_params=pltpu.CompilerParams(vmem_limit_bytes=32 << 20),
        name="local",
    )(*operands, rim)
    pair = lax.all_gather(totals, "c", axis=0, tiled=False)
    chip = decays[stretches] * pair[0] + pair[1]
    everyone = lax.all_to_all(
        jnp.broadcast_to(chip[None], (zs, modes, chans)), "z", split_axis=0, concat_axis=0, tiled=True
    )
    spread = pl.pallas_call(
        join_kernel,
        out_shape=shape((xs, yh, piece, rows), BF16),
        in_specs=[SMEM] + [VMEM] * 7,
        out_specs=VMEM,
        scratch_shapes=[
            pltpu.VMEM((stretches, modes, chans), F32),
            pltpu.VMEM((rows, chans), F32),
            pltpu.VMEM((modes, TILE, chans), F32),
        ],
        cost_estimate=pl.CostEstimate(flops=4_000_000, bytes_accessed=4_000_000, transcendentals=0),
        compiler_params=pltpu.CompilerParams(vmem_limit_bytes=32 << 20),
        name="join",
    )(place, everyone, pair, before, decays, slope, inner, query)
    gathered = lax.all_to_all(
        spread.reshape(xs * yh, piece, rows), ("x", "yh"), split_axis=0, concat_axis=0, tiled=True
    )
    weights = pltpu.with_memory_space_constraint(weights.reshape(length, splits, height, wide), pltpu.HBM)
    partial = pl.pallas_call(
        project_kernel,
        out_shape=shape((splits, rows, wide), BF16),
        in_specs=[VMEM, pl.BlockSpec(memory_space=pl.ANY)],
        out_specs=VMEM,
        scratch_shapes=[
            pltpu.VMEM((splits // 2, length, height, 2 * wide), BF16),
            pltpu.SemaphoreType.DMA((splits,)),
        ],
        cost_estimate=pl.CostEstimate(
            flops=2 * rows * length * height * wide * splits, bytes_accessed=6_000_000, transcendentals=0
        ),
        compiler_params=pltpu.CompilerParams(vmem_limit_bytes=32 << 20),
        name="project",
    )(gathered, weights)
    shares = lax.all_to_all(partial, DEEP, split_axis=0, concat_axis=0, tiled=True)
    total = shares[0].astype(F32)
    for i in range(1, splits):
        total = total + shares[i].astype(F32)
    return total.astype(BF16)


def solution(mesh):
    cores, xs, yl = SHAPE["c"], SHAPE["x"], SHAPE["yl"]
    yh = mesh.shape["ch"] // (xs * yl)
    fine = Mesh(mesh.devices.reshape(-1, cores, xs, yh, yl), CTX + CH)
    return jax.shard_map(
        mixed_of,
        mesh=fine,
        in_specs=(
            P(None, CTX, CH),
            P(None, None, CH),
            P(CH, None),
            P(CH, None),
            P(CH),
            P(CTX, CH),
        ),
        out_specs=P(CTX, CH),
        check_vma=False,
    )
```

```python
import jax
import jax.numpy as jnp
from jax import lax
from jax.experimental import pallas as pl
from jax.experimental.pallas import tpu as pltpu
from jax.sharding import Mesh
from jax.sharding import PartitionSpec as P


STRETCH = 64
TILE = 8
RIM = 8
SHAPE = {"c": 2, "x": 4, "yl": 2}
F32 = jnp.float32
BF16 = jnp.bfloat16
CTX = ("z", "c")
CH = ("x", "yh", "yl")
DEEP = ("yl", "x")
VMEM = pl.BlockSpec(memory_space=pltpu.VMEM)
SMEM = pl.BlockSpec(memory_space=pltpu.SMEM)


def local_kernel(
    features_at, taps_at, rates_at, gains_at, skip_at, rim, query, inner, before, decays, slope, totals,
    features, taps, rates_in, gains_in, skip, sems, extended, product,
):
    pairs = ((rates_at, rates_in), (gains_at, gains_in), (features_at, features), (taps_at, taps), (skip_at, skip))
    copies = [pltpu.make_async_copy(src, dst, sems.at[i]) for i, (src, dst) in enumerate(pairs)]
    for copy in copies:
        copy.start()
    streams, rows, chans = features.shape
    stretches, modes, _ = before.shape
    width = taps.shape[1]
    for copy in copies[:2]:
        copy.wait()
    rates = rates_in[...]
    gain = gains_in[...]
    for k in range(stretches + 1):
        decays[k] = jnp.exp(-rates * (k * STRETCH))
    decays[stretches + 1] = jnp.exp(-rates * TILE)
    lags = lax.broadcasted_iota(jnp.int32, (TILE, chans), 0).astype(F32) + 1.0
    for n in range(modes):
        slope[n] = gain[n : n + 1, :] * jnp.exp(-rates[n : n + 1, :] * lags)
    for copy in copies[2:]:
        copy.wait()
    through = skip[...]
    piece = 32
    for f in range(streams):
        extended[f, 0:RIM, :] = rim[f].astype(F32)
        extended[f, RIM : RIM + rows, :] = features[f].astype(F32)
    for start in range(0, rows, piece):
        parts = []
        for f in range(streams):
            total = jnp.zeros((piece, chans), F32)
            for offset in range(width):
                at = RIM + start - offset
                total = total + taps[f, offset : offset + 1, :] * extended[f, at : at + piece, :]
            parts.append(total.astype(BF16))
        query[start : start + piece, :] = parts[0]
        product[start : start + piece, :] = (
            (parts[1].astype(F32) * parts[2].astype(F32)).astype(BF16).astype(F32)
        )
    decay = jnp.exp(-rates)

    def eight(i, states):
        states = list(states)
        base = pl.multiple_of(i * TILE, TILE)
        for k in range(stretches):
            at = pl.multiple_of(k * STRETCH + base, TILE)
            tile = product[pl.ds(at, TILE), :]
            outs = []
            state = states[k]
            for r in range(TILE):
                state = decay * state + jnp.broadcast_to(tile[r : r + 1, :], (modes, chans))
                outs.append(jnp.sum(gain * state, axis=0, keepdims=True))
            states[k] = state
            inner[pl.ds(at, TILE), :] = jnp.concatenate(outs, axis=0) + through * tile
        return tuple(states)

    zero = jnp.zeros((modes, chans), F32)
    states = lax.fori_loop(0, STRETCH // TILE, eight, (zero,) * stretches)
    across = decays[1]
    running = zero
    for k in range(stretches):
        before[k] = running
        running = across * running + states[k]
    totals[...] = running


def join_kernel(place, everyone, pair, before, decays, slope, inner, query, out, starts, gated, table):
    chips, modes, chans = everyone.shape
    stretches = before.shape[0]
    span = decays[stretches]
    chip_span = span * span
    incoming = jnp.zeros((modes, chans), F32)
    for i in range(chips):
        incoming = jnp.where(i < place[0], chip_span * incoming + everyone[i], incoming)
    incoming = jnp.where(place[1] > 0, span * incoming + pair[0], incoming)
    for k in range(stretches):
        starts[k] = decays[k] * incoming + before[k]
    table[...] = slope[...]

    def eight(i, carry):
        base = pl.multiple_of(i * TILE, TILE)
        totals = [inner[pl.ds(pl.multiple_of(k * STRETCH + base, TILE), TILE), :] for k in range(stretches)]
        for n in range(modes):
            weight = table[n]
            table[n] = weight * decays[stretches + 1, n : n + 1, :]
            for k in range(stretches):
                totals[k] = totals[k] + weight * starts[k, n : n + 1, :]
        for k in range(stretches):
            at = pl.multiple_of(k * STRETCH + base, TILE)
            gated[pl.ds(at, TILE), :] = query[pl.ds(at, TILE), :].astype(F32) * totals[k]
        return carry

    lax.fori_loop(0, STRETCH // TILE, eight, 0)
    turned = gated[...].T.astype(BF16)
    blocks, copies, height, _ = out.shape
    for b in range(blocks):
        for copy in range(copies):
            out[b, copy] = turned[b * height : (b + 1) * height, :]


def project_kernel(gated, weight_at, out, weight, sems):
    parts = out.shape[0]
    groups, length, height, wide = weight.shape
    share = parts // groups
    single = wide // share
    copies = [
        pltpu.make_async_copy(
            weight_at.at[:, i],
            weight.at[i // share, :, :, pl.ds((i % share) * single, single)],
            sems.at[i],
        )
        for i in range(parts)
    ]
    for copy in copies:
        copy.start()
    depth = length * height
    left = gated[...].reshape(depth, gated.shape[2])
    for i in range(groups):
        for copy in copies[i * share : (i + 1) * share]:
            copy.wait()
        right = weight[i].reshape(depth, wide)
        total = lax.dot_general(left, right, (((0,), (0,)), ((), ())), preferred_element_type=F32)
        for j in range(share):
            out[i * share + j] = total[:, j * single : (j + 1) * single].astype(BF16)


def mixed_of(features, short_weight, rates, residues, skip, out_weight):
    streams, rows, chans = features.shape
    modes = rates.shape[1]
    length = lax.axis_size(CTX)
    zs, xs, yh, yl = (lax.axis_size(name) for name in ("z", "x", "yh", "yl"))
    splits = xs * yl
    place = jnp.stack([lax.axis_index("z"), lax.axis_index("c")]).astype(jnp.int32)
    decay_rate = rates.T
    mode_gain = residues.T
    shape = jax.ShapeDtypeStruct

    deep, wide = out_weight.shape
    piece = chans // xs
    height = deep // splits
    sliced = out_weight.reshape(splits, height, wide)
    sliced = lax.all_to_all(sliced, DEEP, split_axis=0, concat_axis=0, tiled=True)

    edge = features[:, rows - RIM :, :]
    rim = lax.ppermute(edge, CTX, [(i, i + 1) for i in range(length - 1)])
    rim, place, sliced = lax.optimization_barrier((rim, place, sliced))
    weights = lax.all_gather(sliced, CTX, axis=0, tiled=False)

    stretches = rows // STRETCH
    shapes = (
        shape((rows, chans), BF16),
        shape((rows, chans), F32),
        shape((stretches, modes, chans), F32),
        shape((stretches + 2, modes, chans), F32),
        shape((modes, TILE, chans), F32),
        shape((modes, chans), F32),
    )
    operands = (features, short_weight, decay_rate, mode_gain, skip[None, :])
    operands = tuple(pltpu.with_memory_space_constraint(v, pltpu.HBM) for v in operands)
    query, inner, before, decays, slope, totals = pl.pallas_call(
        local_kernel,
        out_shape=shapes,
        in_specs=[pl.BlockSpec(memory_space=pltpu.HBM)] * len(operands) + [VMEM],
        out_specs=(VMEM,) * len(shapes),
        scratch_shapes=[pltpu.VMEM(v.shape, v.dtype) for v in operands]
        + [
            pltpu.SemaphoreType.DMA((len(operands),)),
            pltpu.VMEM((streams, rows + RIM, chans), F32),
            pltpu.VMEM((rows, chans), F32),
        ],
        cost_estimate=pl.CostEstimate(flops=8_000_000, bytes_accessed=2_000_000, transcendentals=0),
        compiler_params=pltpu.CompilerParams(vmem_limit_bytes=32 << 20),
        name="local",
    )(*operands, rim)
    pair = lax.all_gather(totals, "c", axis=0, tiled=False)
    chip = decays[stretches] * pair[0] + pair[1]
    everyone = lax.all_to_all(
        jnp.broadcast_to(chip[None], (zs, modes, chans)), "z", split_axis=0, concat_axis=0, tiled=True
    )
    spread = pl.pallas_call(
        join_kernel,
        out_shape=shape((xs, yh, piece, rows), BF16),
        in_specs=[SMEM] + [VMEM] * 7,
        out_specs=VMEM,
        scratch_shapes=[
            pltpu.VMEM((stretches, modes, chans), F32),
            pltpu.VMEM((rows, chans), F32),
            pltpu.VMEM((modes, TILE, chans), F32),
        ],
        cost_estimate=pl.CostEstimate(flops=4_000_000, bytes_accessed=4_000_000, transcendentals=0),
        compiler_params=pltpu.CompilerParams(vmem_limit_bytes=32 << 20),
        name="join",
    )(place, everyone, pair, before, decays, slope, inner, query)
    gathered = lax.all_to_all(
        spread.reshape(xs * yh, piece, rows), ("x", "yh"), split_axis=0, concat_axis=0, tiled=True
    )
    weights = pltpu.with_memory_space_constraint(weights.reshape(length, splits, height, wide), pltpu.HBM)
    partial = pl.pallas_call(
        project_kernel,
        out_shape=shape((splits, rows, wide), BF16),
        in_specs=[VMEM, pl.BlockSpec(memory_space=pl.ANY)],
        out_specs=VMEM,
        scratch_shapes=[
            pltpu.VMEM((splits // 2, length, height, 2 * wide), BF16),
            pltpu.SemaphoreType.DMA((splits,)),
        ],
        cost_estimate=pl.CostEstimate(
            flops=2 * rows * length * height * wide * splits, bytes_accessed=6_000_000, transcendentals=0
        ),
        compiler_params=pltpu.CompilerParams(vmem_limit_bytes=32 << 20),
        name="project",
    )(gathered, weights)
    shares = lax.all_to_all(partial, DEEP, split_axis=0, concat_axis=0, tiled=True)
    total = shares[0].astype(F32)
    for i in range(1, splits):
        total = total + shares[i].astype(F32)
    return total.astype(BF16)


def solution(mesh):
    cores, xs, yl = SHAPE["c"], SHAPE["x"], SHAPE["yl"]
    yh = mesh.shape["ch"] // (xs * yl)
    fine = Mesh(mesh.devices.reshape(-1, cores, xs, yh, yl), CTX + CH)
    return jax.shard_map(
        mixed_of,
        mesh=fine,
        in_specs=(
            P(None, CTX, CH),
            P(None, None, CH),
            P(CH, None),
            P(CH, None),
            P(CH),
            P(CTX, CH),
        ),
        out_specs=P(CTX, CH),
        check_vma=False,
    )
```

```python
import jax
import jax.numpy as jnp
from jax import lax
from jax.experimental import pallas as pl
from jax.experimental.pallas import tpu as pltpu
from jax.sharding import Mesh
from jax.sharding import PartitionSpec as P


STRETCH = 64
TILE = 8
RIM = 8
SHAPE = {"c": 2, "x": 4, "yl": 2}
F32 = jnp.float32
BF16 = jnp.bfloat16
CTX = ("z", "c")
CH = ("x", "yh", "yl")
DEEP = ("yl", "x")
VMEM = pl.BlockSpec(memory_space=pltpu.VMEM)
SMEM = pl.BlockSpec(memory_space=pltpu.SMEM)


def local_kernel(
    features_at, taps_at, rates_at, gains_at, skip_at, rim, query, inner, before, decays, slope, totals,
    features, taps, rates_in, gains_in, skip, sems, extended, product,
):
    pairs = ((rates_at, rates_in), (gains_at, gains_in), (features_at, features), (taps_at, taps), (skip_at, skip))
    copies = [pltpu.make_async_copy(src, dst, sems.at[i]) for i, (src, dst) in enumerate(pairs)]
    for copy in copies:
        copy.start()
    streams, rows, chans = features.shape
    stretches, modes, _ = before.shape
    width = taps.shape[1]
    for copy in copies[:2]:
        copy.wait()
    rates = rates_in[...]
    gain = gains_in[...]
    for k in range(stretches + 1):
        decays[k] = jnp.exp(-rates * (k * STRETCH))
    decays[stretches + 1] = jnp.exp(-rates * TILE)
    lags = lax.broadcasted_iota(jnp.int32, (TILE, chans), 0).astype(F32) + 1.0
    for n in range(modes):
        slope[n] = gain[n : n + 1, :] * jnp.exp(-rates[n : n + 1, :] * lags)
    for copy in copies[2:]:
        copy.wait()
    through = skip[...]
    piece = 32
    for f in range(streams):
        extended[f, 0:RIM, :] = rim[f].astype(F32)
        extended[f, RIM : RIM + rows, :] = features[f].astype(F32)
    for start in range(0, rows, piece):
        parts = []
        for f in range(streams):
            total = jnp.zeros((piece, chans), F32)
            for offset in range(width):
                at = RIM + start - offset
                total = total + taps[f, offset : offset + 1, :] * extended[f, at : at + piece, :]
            parts.append(total.astype(BF16))
        query[start : start + piece, :] = parts[0]
        product[start : start + piece, :] = (
            (parts[1].astype(F32) * parts[2].astype(F32)).astype(BF16).astype(F32)
        )
    decay = jnp.exp(-rates)

    def eight(i, states):
        states = list(states)
        base = pl.multiple_of(i * TILE, TILE)
        for k in range(stretches):
            at = pl.multiple_of(k * STRETCH + base, TILE)
            tile = product[pl.ds(at, TILE), :]
            outs = []
            state = states[k]
            for r in range(TILE):
                state = decay * state + jnp.broadcast_to(tile[r : r + 1, :], (modes, chans))
                outs.append(jnp.sum(gain * state, axis=0, keepdims=True))
            states[k] = state
            inner[pl.ds(at, TILE), :] = jnp.concatenate(outs, axis=0) + through * tile
        return tuple(states)

    zero = jnp.zeros((modes, chans), F32)
    states = lax.fori_loop(0, STRETCH // TILE, eight, (zero,) * stretches)
    across = decays[1]
    running = zero
    for k in range(stretches):
        before[k] = running
        running = across * running + states[k]
    totals[...] = running


def join_kernel(place, everyone, pair, before, decays, slope, inner, query, out, starts, gated, table):
    chips, modes, chans = everyone.shape
    stretches = before.shape[0]
    span = decays[stretches]
    chip_span = span * span
    incoming = jnp.zeros((modes, chans), F32)
    for i in range(chips):
        incoming = jnp.where(i < place[0], chip_span * incoming + everyone[i], incoming)
    incoming = jnp.where(place[1] > 0, span * incoming + pair[0], incoming)
    for k in range(stretches):
        starts[k] = decays[k] * incoming + before[k]
    table[...] = slope[...]

    def eight(i, carry):
        base = pl.multiple_of(i * TILE, TILE)
        totals = [inner[pl.ds(pl.multiple_of(k * STRETCH + base, TILE), TILE), :] for k in range(stretches)]
        for n in range(modes):
            weight = table[n]
            table[n] = weight * decays[stretches + 1, n : n + 1, :]
            for k in range(stretches):
                totals[k] = totals[k] + weight * starts[k, n : n + 1, :]
        for k in range(stretches):
            at = pl.multiple_of(k * STRETCH + base, TILE)
            gated[pl.ds(at, TILE), :] = query[pl.ds(at, TILE), :].astype(F32) * totals[k]
        return carry

    lax.fori_loop(0, STRETCH // TILE, eight, 0)
    turned = gated[...].T.astype(BF16)
    blocks, copies, height, _ = out.shape
    for b in range(blocks):
        for copy in range(copies):
            out[b, copy] = turned[b * height : (b + 1) * height, :]


def project_kernel(gated, weight_at, out, weight, sems):
    parts = out.shape[0]
    groups, length, height, wide = weight.shape
    share = parts // groups
    single = wide // share
    cuts = 4
    run = length // cuts
    copies = [
        pltpu.make_async_copy(
            weight_at.at[pl.ds(k * run, run), i],
            weight.at[i // share, pl.ds(k * run, run), :, pl.ds((i % share) * single, single)],
            sems.at[i, k],
        )
        for i in range(parts)
        for k in range(cuts)
    ]
    for copy in copies:
        copy.start()
    depth = length * height
    left = gated[...].reshape(depth, gated.shape[2])
    for i in range(groups):
        for copy in copies[i * share * cuts : (i + 1) * share * cuts]:
            copy.wait()
        right = weight[i].reshape(depth, wide)
        total = lax.dot_general(left, right, (((0,), (0,)), ((), ())), preferred_element_type=F32)
        for j in range(share):
            out[i * share + j] = total[:, j * single : (j + 1) * single].astype(BF16)


def mixed_of(features, short_weight, rates, residues, skip, out_weight):
    streams, rows, chans = features.shape
    modes = rates.shape[1]
    length = lax.axis_size(CTX)
    zs, xs, yh, yl = (lax.axis_size(name) for name in ("z", "x", "yh", "yl"))
    splits = xs * yl
    place = jnp.stack([lax.axis_index("z"), lax.axis_index("c")]).astype(jnp.int32)
    decay_rate = rates.T
    mode_gain = residues.T
    shape = jax.ShapeDtypeStruct

    deep, wide = out_weight.shape
    piece = chans // xs
    height = deep // splits
    sliced = out_weight.reshape(splits, height, wide)
    sliced = lax.all_to_all(sliced, DEEP, split_axis=0, concat_axis=0, tiled=True)

    edge = features[:, rows - RIM :, :]
    rim = lax.ppermute(edge, CTX, [(i, i + 1) for i in range(length - 1)])
    rim, place, sliced = lax.optimization_barrier((rim, place, sliced))
    weights = lax.all_gather(sliced, CTX, axis=0, tiled=False)

    stretches = rows // STRETCH
    shapes = (
        shape((rows, chans), BF16),
        shape((rows, chans), F32),
        shape((stretches, modes, chans), F32),
        shape((stretches + 2, modes, chans), F32),
        shape((modes, TILE, chans), F32),
        shape((modes, chans), F32),
    )
    operands = (features, short_weight, decay_rate, mode_gain, skip[None, :])
    operands = tuple(pltpu.with_memory_space_constraint(v, pltpu.HBM) for v in operands)
    query, inner, before, decays, slope, totals = pl.pallas_call(
        local_kernel,
        out_shape=shapes,
        in_specs=[pl.BlockSpec(memory_space=pltpu.HBM)] * len(operands) + [VMEM],
        out_specs=(VMEM,) * len(shapes),
        scratch_shapes=[pltpu.VMEM(v.shape, v.dtype) for v in operands]
        + [
            pltpu.SemaphoreType.DMA((len(operands),)),
            pltpu.VMEM((streams, rows + RIM, chans), F32),
            pltpu.VMEM((rows, chans), F32),
        ],
        cost_estimate=pl.CostEstimate(flops=8_000_000, bytes_accessed=2_000_000, transcendentals=0),
        compiler_params=pltpu.CompilerParams(vmem_limit_bytes=32 << 20),
        name="local",
    )(*operands, rim)
    pair = lax.all_gather(totals, "c", axis=0, tiled=False)
    chip = decays[stretches] * pair[0] + pair[1]
    everyone = lax.all_to_all(
        jnp.broadcast_to(chip[None], (zs, modes, chans)), "z", split_axis=0, concat_axis=0, tiled=True
    )
    spread = pl.pallas_call(
        join_kernel,
        out_shape=shape((xs, yh, piece, rows), BF16),
        in_specs=[SMEM] + [VMEM] * 7,
        out_specs=VMEM,
        scratch_shapes=[
            pltpu.VMEM((stretches, modes, chans), F32),
            pltpu.VMEM((rows, chans), F32),
            pltpu.VMEM((modes, TILE, chans), F32),
        ],
        cost_estimate=pl.CostEstimate(flops=4_000_000, bytes_accessed=4_000_000, transcendentals=0),
        compiler_params=pltpu.CompilerParams(vmem_limit_bytes=32 << 20),
        name="join",
    )(place, everyone, pair, before, decays, slope, inner, query)
    gathered = lax.all_to_all(
        spread.reshape(xs * yh, piece, rows), ("x", "yh"), split_axis=0, concat_axis=0, tiled=True
    )
    weights = pltpu.with_memory_space_constraint(weights.reshape(length, splits, height, wide), pltpu.HBM)
    partial = pl.pallas_call(
        project_kernel,
        out_shape=shape((splits, rows, wide), BF16),
        in_specs=[VMEM, pl.BlockSpec(memory_space=pl.ANY)],
        out_specs=VMEM,
        scratch_shapes=[
            pltpu.VMEM((splits // 2, length, height, 2 * wide), BF16),
            pltpu.SemaphoreType.DMA((splits, 4)),
        ],
        cost_estimate=pl.CostEstimate(
            flops=2 * rows * length * height * wide * splits, bytes_accessed=6_000_000, transcendentals=0
        ),
        compiler_params=pltpu.CompilerParams(vmem_limit_bytes=32 << 20),
        name="project",
    )(gathered, weights)
    shares = lax.all_to_all(partial, DEEP, split_axis=0, concat_axis=0, tiled=True)
    total = shares[0].astype(F32)
    for i in range(1, splits):
        total = total + shares[i].astype(F32)
    return total.astype(BF16)


def solution(mesh):
    cores, xs, yl = SHAPE["c"], SHAPE["x"], SHAPE["yl"]
    yh = mesh.shape["ch"] // (xs * yl)
    fine = Mesh(mesh.devices.reshape(-1, cores, xs, yh, yl), CTX + CH)
    return jax.shard_map(
        mixed_of,
        mesh=fine,
        in_specs=(
            P(None, CTX, CH),
            P(None, None, CH),
            P(CH, None),
            P(CH, None),
            P(CH),
            P(CTX, CH),
        ),
        out_specs=P(CTX, CH),
        check_vma=False,
    )
```

```python
import jax
import jax.numpy as jnp
from jax import lax
from jax.experimental import pallas as pl
from jax.experimental.pallas import tpu as pltpu
from jax.sharding import Mesh
from jax.sharding import PartitionSpec as P


STRETCH = 64
TILE = 8
RIM = 8
SHAPE = {"c": 2, "x": 4, "yl": 2}
F32 = jnp.float32
BF16 = jnp.bfloat16
CTX = ("z", "c")
CH = ("x", "yh", "yl")
DEEP = ("yl", "x")
VMEM = pl.BlockSpec(memory_space=pltpu.VMEM)
SMEM = pl.BlockSpec(memory_space=pltpu.SMEM)


def local_kernel(
    features_at, taps_at, rates_at, gains_at, skip_at, rim, query, inner, before, decays, slope, totals,
    features, taps, rates_in, gains_in, skip, sems, extended, product,
):
    pairs = ((rates_at, rates_in), (gains_at, gains_in), (features_at, features), (taps_at, taps), (skip_at, skip))
    copies = [pltpu.make_async_copy(src, dst, sems.at[i]) for i, (src, dst) in enumerate(pairs)]
    for copy in copies:
        copy.start()
    streams, rows, chans = features.shape
    stretches, modes, _ = before.shape
    width = taps.shape[1]
    for copy in copies[:2]:
        copy.wait()
    rates = rates_in[...]
    gain = gains_in[...]
    for k in range(stretches + 1):
        decays[k] = jnp.exp(-rates * (k * STRETCH))
    decays[stretches + 1] = jnp.exp(-rates * TILE)
    lags = lax.broadcasted_iota(jnp.int32, (TILE, chans), 0).astype(F32) + 1.0
    for n in range(modes):
        slope[n] = gain[n : n + 1, :] * jnp.exp(-rates[n : n + 1, :] * lags)
    for copy in copies[2:]:
        copy.wait()
    through = skip[...]
    piece = 32
    for f in range(streams):
        extended[f, 0:RIM, :] = rim[f].astype(F32)
        extended[f, RIM : RIM + rows, :] = features[f].astype(F32)
    for start in range(0, rows, piece):
        parts = []
        for f in range(streams):
            total = jnp.zeros((piece, chans), F32)
            for offset in range(width):
                at = RIM + start - offset
                total = total + taps[f, offset : offset + 1, :] * extended[f, at : at + piece, :]
            parts.append(total.astype(BF16))
        query[start : start + piece, :] = parts[0]
        product[start : start + piece, :] = (
            (parts[1].astype(F32) * parts[2].astype(F32)).astype(BF16).astype(F32)
        )
    decay = jnp.exp(-rates)

    def eight(i, states):
        states = list(states)
        base = pl.multiple_of(i * TILE, TILE)
        for k in range(stretches):
            at = pl.multiple_of(k * STRETCH + base, TILE)
            tile = product[pl.ds(at, TILE), :]
            outs = []
            state = states[k]
            for r in range(TILE):
                state = decay * state + jnp.broadcast_to(tile[r : r + 1, :], (modes, chans))
                outs.append(jnp.sum(gain * state, axis=0, keepdims=True))
            states[k] = state
            inner[pl.ds(at, TILE), :] = jnp.concatenate(outs, axis=0) + through * tile
        return tuple(states)

    zero = jnp.zeros((modes, chans), F32)
    states = lax.fori_loop(0, STRETCH // TILE, eight, (zero,) * stretches)
    across = decays[1]
    running = zero
    for k in range(stretches):
        before[k] = running
        running = across * running + states[k]
    totals[...] = running


def join_kernel(place, everyone, pair, before, decays, slope, inner, query, out, starts, gated, table):
    chips, modes, chans = everyone.shape
    stretches = before.shape[0]
    span = decays[stretches]
    chip_span = span * span
    incoming = jnp.zeros((modes, chans), F32)
    for i in range(chips):
        incoming = jnp.where(i < place[0], chip_span * incoming + everyone[i], incoming)
    incoming = jnp.where(place[1] > 0, span * incoming + pair[0], incoming)
    for k in range(stretches):
        starts[k] = decays[k] * incoming + before[k]
    table[...] = slope[...]

    def eight(i, carry):
        base = pl.multiple_of(i * TILE, TILE)
        totals = [inner[pl.ds(pl.multiple_of(k * STRETCH + base, TILE), TILE), :] for k in range(stretches)]
        for n in range(modes):
            weight = table[n]
            table[n] = weight * decays[stretches + 1, n : n + 1, :]
            for k in range(stretches):
                totals[k] = totals[k] + weight * starts[k, n : n + 1, :]
        for k in range(stretches):
            at = pl.multiple_of(k * STRETCH + base, TILE)
            gated[pl.ds(at, TILE), :] = query[pl.ds(at, TILE), :].astype(F32) * totals[k]
        return carry

    lax.fori_loop(0, STRETCH // TILE, eight, 0)
    turned = gated[...].T.astype(BF16)
    blocks, copies, height, _ = out.shape
    for b in range(blocks):
        for copy in range(copies):
            out[b, copy] = turned[b * height : (b + 1) * height, :]


def project_kernel(gated, weight_at, out, weight, sems):
    parts = out.shape[0]
    groups, length, height, wide = weight.shape
    share = parts // groups
    single = wide // share
    copies = [
        pltpu.make_async_copy(
            weight_at.at[:, i],
            weight.at[i // share, :, :, pl.ds((i % share) * single, single)],
            sems.at[i],
        )
        for i in range(parts)
    ]
    for copy in copies:
        copy.start()
    depth = length * height
    left = gated[...].reshape(depth, gated.shape[2])
    for i in range(groups):
        for copy in copies[i * share : (i + 1) * share]:
            copy.wait()
        right = weight[i].reshape(depth, wide)
        total = lax.dot_general(left, right, (((0,), (0,)), ((), ())), preferred_element_type=F32)
        for j in range(share):
            out[i * share + j] = total[:, j * single : (j + 1) * single].astype(BF16)


def mixed_of(features, short_weight, rates, residues, skip, out_weight):
    streams, rows, chans = features.shape
    modes = rates.shape[1]
    length = lax.axis_size(CTX)
    zs, xs, yh, yl = (lax.axis_size(name) for name in ("z", "x", "yh", "yl"))
    splits = xs * yl
    decay_rate = rates.T
    mode_gain = residues.T
    shape = jax.ShapeDtypeStruct

    deep, wide = out_weight.shape
    piece = chans // xs
    height = deep // splits
    sliced = out_weight.reshape(splits, height, wide)
    sliced = lax.all_to_all(sliced, DEEP, split_axis=0, concat_axis=0, tiled=True)

    edge = features[:, rows - RIM :, :]
    rim = lax.ppermute(edge, CTX, [(i, i + 1) for i in range(length - 1)])
    seat, sliced = lax.optimization_barrier(((lax.axis_index("z"), lax.axis_index("c")), sliced))
    place = jnp.stack(seat).astype(jnp.int32)
    rim, place = lax.optimization_barrier((rim, place))
    weights = lax.all_gather(sliced, CTX, axis=0, tiled=False)

    stretches = rows // STRETCH
    shapes = (
        shape((rows, chans), BF16),
        shape((rows, chans), F32),
        shape((stretches, modes, chans), F32),
        shape((stretches + 2, modes, chans), F32),
        shape((modes, TILE, chans), F32),
        shape((modes, chans), F32),
    )
    operands = (features, short_weight, decay_rate, mode_gain, skip[None, :])
    operands = tuple(pltpu.with_memory_space_constraint(v, pltpu.HBM) for v in operands)
    query, inner, before, decays, slope, totals = pl.pallas_call(
        local_kernel,
        out_shape=shapes,
        in_specs=[pl.BlockSpec(memory_space=pltpu.HBM)] * len(operands) + [VMEM],
        out_specs=(VMEM,) * len(shapes),
        scratch_shapes=[pltpu.VMEM(v.shape, v.dtype) for v in operands]
        + [
            pltpu.SemaphoreType.DMA((len(operands),)),
            pltpu.VMEM((streams, rows + RIM, chans), F32),
            pltpu.VMEM((rows, chans), F32),
        ],
        cost_estimate=pl.CostEstimate(flops=8_000_000, bytes_accessed=2_000_000, transcendentals=0),
        compiler_params=pltpu.CompilerParams(vmem_limit_bytes=32 << 20),
        name="local",
    )(*operands, rim)
    pair = lax.all_gather(totals, "c", axis=0, tiled=False)
    chip = decays[stretches] * pair[0] + pair[1]
    everyone = lax.all_to_all(
        jnp.broadcast_to(chip[None], (zs, modes, chans)), "z", split_axis=0, concat_axis=0, tiled=True
    )
    spread = pl.pallas_call(
        join_kernel,
        out_shape=shape((xs, yh, piece, rows), BF16),
        in_specs=[SMEM] + [VMEM] * 7,
        out_specs=VMEM,
        scratch_shapes=[
            pltpu.VMEM((stretches, modes, chans), F32),
            pltpu.VMEM((rows, chans), F32),
            pltpu.VMEM((modes, TILE, chans), F32),
        ],
        cost_estimate=pl.CostEstimate(flops=4_000_000, bytes_accessed=4_000_000, transcendentals=0),
        compiler_params=pltpu.CompilerParams(vmem_limit_bytes=32 << 20),
        name="join",
    )(place, everyone, pair, before, decays, slope, inner, query)
    gathered = lax.all_to_all(
        spread.reshape(xs * yh, piece, rows), ("x", "yh"), split_axis=0, concat_axis=0, tiled=True
    )
    weights = pltpu.with_memory_space_constraint(weights.reshape(length, splits, height, wide), pltpu.HBM)
    partial = pl.pallas_call(
        project_kernel,
        out_shape=shape((splits, rows, wide), BF16),
        in_specs=[VMEM, pl.BlockSpec(memory_space=pl.ANY)],
        out_specs=VMEM,
        scratch_shapes=[
            pltpu.VMEM((splits // 2, length, height, 2 * wide), BF16),
            pltpu.SemaphoreType.DMA((splits,)),
        ],
        cost_estimate=pl.CostEstimate(
            flops=2 * rows * length * height * wide * splits, bytes_accessed=6_000_000, transcendentals=0
        ),
        compiler_params=pltpu.CompilerParams(vmem_limit_bytes=32 << 20),
        name="project",
    )(gathered, weights)
    shares = lax.all_to_all(partial, DEEP, split_axis=0, concat_axis=0, tiled=True)
    total = shares[0].astype(F32)
    for i in range(1, splits):
        total = total + shares[i].astype(F32)
    return total.astype(BF16)


def solution(mesh):
    cores, xs, yl = SHAPE["c"], SHAPE["x"], SHAPE["yl"]
    yh = mesh.shape["ch"] // (xs * yl)
    fine = Mesh(mesh.devices.reshape(-1, cores, xs, yh, yl), CTX + CH)
    return jax.shard_map(
        mixed_of,
        mesh=fine,
        in_specs=(
            P(None, CTX, CH),
            P(None, None, CH),
            P(CH, None),
            P(CH, None),
            P(CH),
            P(CTX, CH),
        ),
        out_specs=P(CTX, CH),
        check_vma=False,
    )
```
